512 devices in a mesh: dp: 8 (over z_hi, x), seq: 64 (over z_lo, y, core).
Axes of the slice: x: 4, y: 4, z: 16 (z_hi: 2, z_lo: 8; z = z_hi * 8 + z_lo), core: 2. Of those that a mesh axis runs over, the one named last changes fastest.
Arguments:
- queries: bfloat16 [32768, 2048], P('seq', 'dp'), may hold values from -15 to 15
- key_rows: bfloat16 [32768, 2048], P('seq', 'dp'), may hold values from -15 to 15
- value_rows: bfloat16 [32768, 2048], P('seq', 'dp'), may hold values from -6 to 6
- slot_queries: bfloat16 [256, 2048], P(None, 'dp'), may hold values from -15 to 15
- gate_logit: float32 [64, 2048], P('seq', 'dp'), may hold values from -6.5 to 6.5
- out_weight: bfloat16 [2048, 2048], P(None, 'dp'), may hold values from -0.1875 to 0.1875
Outputs:
- mixed: bfloat16 [2048, 32768], P('dp', 'seq')
The draws below stay inside these ranges and needn't reach their ends.
All inputs are finite; a program needn't handle non-finite values.
Results may differ from the reference program's by a relative error of at most 0.017.
Values may be sent and summed in bfloat16 or wider, within the bound.
A program may use at most 64 MiB of HBM per device.

```python
import jax
import jax.numpy as jnp
from jax import lax

HEADS = 16
HEAD = 128
STATE = 256
TOK_DEV = 512
FEATURE_SPAN = 2048
OUT_WIDTH = 2048
SEGMENTS_IN_TOME = 64
LENGTH = 32768


def loguniform_draw(seed_key, shape, low_end, high_end):
    return jnp.exp(jax.random.uniform(seed_key, shape, jnp.float32, jnp.log(low_end), jnp.log(high_end)))


def draw_queries(key, part):
    noise_key = jax.random.fold_in(key, 11)
    values = jax.random.truncated_normal(noise_key, -4.0, 4.0, (LENGTH, FEATURE_SPAN), jnp.float32)
    return values.astype(jnp.bfloat16)


def draw_key_rows(key, part):
    noise_key = jax.random.fold_in(key, 12)
    values = jax.random.truncated_normal(noise_key, -4.0, 4.0, (LENGTH, FEATURE_SPAN), jnp.float32)
    return values.astype(jnp.bfloat16)


def draw_slot_queries(key, part):
    noise_key = jax.random.fold_in(key, 13)
    values = jax.random.truncated_normal(noise_key, -4.0, 4.0, (STATE, FEATURE_SPAN), jnp.float32)
    return values.astype(jnp.bfloat16)


def draw_gate_logit(key, part):
    slow_share = 0.5
    slow_heads = jax.random.bernoulli(jax.random.fold_in(key, 21), slow_share, (1, HEADS))
    lingering = jnp.repeat(slow_heads, HEAD, axis=1)
    slow_decay = jnp.log(10.0) / SEGMENTS_IN_TOME * loguniform_draw(jax.random.fold_in(key, 22), (1, FEATURE_SPAN), 0.2, 0.6)
    fast_decay = loguniform_draw(jax.random.fold_in(key, 23), (1, FEATURE_SPAN), 1.0, 3.0)
    wobble = loguniform_draw(jax.random.fold_in(key, 24), (SEGMENTS_IN_TOME, FEATURE_SPAN), 0.5, 2.0)
    fading = jnp.where(lingering, slow_decay, fast_decay) * wobble
    sudden = jax.random.bernoulli(jax.random.fold_in(key, 25), min(1.0, 3.0 / SEGMENTS_IN_TOME), (SEGMENTS_IN_TOME, 1))
    survival = jax.random.uniform(jax.random.fold_in(key, 26), (SEGMENTS_IN_TOME, FEATURE_SPAN), jnp.float32, 0.5, 0.8)
    persisting = jnp.exp(-fading) * jnp.where(lingering & sudden, survival, 1.0)
    return jnp.log(persisting) - jnp.log1p(-persisting)


def with_spikes(array, stream_key, source, target, shards_of, factor):
    def block_of(axis_at):
        return (jnp.arange(array.shape[axis_at]) // (array.shape[axis_at] // shards_of)).reshape((-1,) + (1,) * (array.ndim - 1 - axis_at))

    first = jax.random.permutation(stream_key, shards_of)[block_of(target)]
    far = (block_of(target) + shards_of // 2) % shards_of
    return jnp.where((block_of(source) == first) | (block_of(source) == far), factor * array, array)


def steps_of(key, dims, cuts, low, top_value):
    def one(axis_at, blocks):
        heights = jax.random.uniform(jax.random.fold_in(jax.random.fold_in(key, 6), axis_at), (blocks,), jnp.float32, low / len(cuts), top_value / len(cuts))
        return jnp.repeat(jnp.exp(heights), dims[axis_at] // blocks).reshape((-1,) + (1,) * (len(dims) - axis_at - 1))

    gain = one(*cuts[0])
    for cut in cuts[1:]:
        gain = gain * one(*cut)
    return gain


def noise(own_key, shape, scale, limit, pieces=(), held_as=jnp.bfloat16):
    factor_of = steps_of(own_key, shape, pieces, -0.22, 0.18) if pieces else 1.0
    entries = jax.random.normal(own_key, shape, jnp.float32) * scale * factor_of
    return jnp.minimum(jnp.maximum(entries, -limit), limit).astype(held_as)


def noise_with(rng, shape, deviation, limit, pieces, heavy, kind=jnp.bfloat16):
    array = deviation * jax.random.normal(rng, shape, jnp.float32)
    if pieces:
        array = array * steps_of(rng, shape, pieces, -0.22, 0.18)
    return jnp.clip(with_spikes(array, jax.random.fold_in(rng, 3), *heavy), -limit, limit).astype(kind)


def setup_inputs(seed: int = 0) -> dict:
    splits = jax.random.split(jax.random.key(seed), 7)
    return {
        "queries": draw_queries(jax.random.fold_in(splits[6], 71), 0),
        "key_rows": draw_key_rows(jax.random.fold_in(splits[6], 71), 0),
        "value_rows": noise(splits[2], (LENGTH, FEATURE_SPAN), 1.0, 6.0, ((0, 64), (1, 8))),
        "slot_queries": draw_slot_queries(jax.random.fold_in(splits[6], 71), 0),
        "gate_logit": draw_gate_logit(jax.random.fold_in(splits[6], 71), 0),
        "out_weight": noise_with(splits[5], (OUT_WIDTH, FEATURE_SPAN), FEATURE_SPAN ** -0.5, 0.1875, ((1, 8),), (1, 0, 8, 2.0)),
    }


def attend(query_part, key_part, value_part, allowed):
    row_count = query_part.shape[0]
    key_count = key_part.shape[0]
    head_count = query_part.shape[1] // HEAD
    queries = query_part.astype(jnp.float32).reshape(row_count, head_count, HEAD)
    keyset = key_part.astype(jnp.float32).reshape(key_count, head_count, HEAD)
    valset = value_part.astype(jnp.float32).reshape(key_count, head_count, HEAD)
    scores = jnp.einsum("rhe,she->hrs", queries, keyset) * (HEAD ** -0.5)
    scores = jnp.where(allowed[None], scores, -1e30)
    highest = jnp.max(scores, axis=-1, keepdims=True)
    weights = jnp.exp(scores - highest)
    totals = jnp.sum(weights, axis=-1, keepdims=True)
    rounded = lax.optimization_barrier(weights.astype(jnp.bfloat16)).astype(jnp.float32)
    summed = jnp.einsum("hrs,she->rhe", rounded, valset)
    return (summed / jnp.transpose(totals, (1, 0, 2))).reshape(row_count, head_count * HEAD)


def token_mask(later_block):
    row_index = lax.broadcasted_iota(jnp.int32, (TOK_DEV, TOK_DEV), 0)
    col_index = lax.broadcasted_iota(jnp.int32, (TOK_DEV, TOK_DEV), 1)
    state_cols = jnp.ones((TOK_DEV, STATE), jnp.bool_)
    return jnp.concatenate([state_cols, (col_index > row_index) & later_block, col_index <= row_index], axis=1)


def read_block(query_block, memory, key_before, value_before, key_block, value_block, allowed):
    memory_wide = lax.optimization_barrier(memory)
    key_all = jnp.concatenate([memory_wide, key_before, key_block], axis=0)
    value_all = jnp.concatenate([memory_wide, value_before, value_block], axis=0)
    group_width = query_block.shape[1] // 4
    results = []
    for group_index in range(4):
        first_col = group_index * group_width
        last_col = first_col + group_width
        results.append(attend(query_block[:, first_col:last_col], key_all[:, first_col:last_col], value_all[:, first_col:last_col], allowed))
    return jnp.concatenate(results, axis=1).astype(jnp.bfloat16)


def reference(queries, key_rows, value_rows, slot_queries, gate_logit, out_weight):
    retention = jax.nn.sigmoid(gate_logit)
    slot_mask = jnp.ones((STATE, TOK_DEV), jnp.bool_)
    key_blocks = key_rows.reshape(SEGMENTS_IN_TOME, TOK_DEV, FEATURE_SPAN)
    value_blocks = value_rows.reshape(SEGMENTS_IN_TOME, TOK_DEV, FEATURE_SPAN)
    query_blocks = queries.reshape(SEGMENTS_IN_TOME, TOK_DEV, FEATURE_SPAN)

    def slot_update(block_inputs):
        return attend(slot_queries, block_inputs[0], block_inputs[1], slot_mask)

    updates = lax.map(slot_update, (key_blocks, value_blocks))

    def advance(carried, step_inputs):
        keep_rate, update = step_inputs
        return keep_rate * carried + (1.0 - keep_rate) * update, carried

    initial = jnp.zeros((STATE, FEATURE_SPAN), jnp.float32)
    final_state, states = lax.scan(advance, initial, (retention, updates))
    memories = states.astype(jnp.bfloat16)
    keys_before = jnp.concatenate([jnp.zeros_like(key_blocks[:1]), key_blocks[:-1]], axis=0)
    values_before = jnp.concatenate([jnp.zeros_like(value_blocks[:1]), value_blocks[:-1]], axis=0)
    block_ids = jnp.arange(SEGMENTS_IN_TOME, dtype=jnp.int32)

    def read_one(step_inputs):
        query_block, memory, key_before, value_before, key_block, value_block, block_id = step_inputs
        return read_block(query_block, memory, key_before, value_before, key_block, value_block, token_mask(block_id > 0))

    attended = lax.map(read_one, (query_blocks, memories, keys_before, values_before, key_blocks, value_blocks, block_ids))
    attended = attended.reshape(LENGTH, FEATURE_SPAN)
    projected = lax.dot_general(out_weight, attended, (((1,), (1,)), ((), ())), preferred_element_type=jnp.float32)
    return projected.astype(jnp.bfloat16)
```

```python
import functools

import jax
import jax.numpy as jnp
from jax import lax
from jax.experimental import pallas as pl
from jax.experimental.pallas import tpu as pltpu
from jax.sharding import PartitionSpec as P

HEAD = 128
MESH = pl.DeviceIdType.MESH
XS, YS, ZLO, ZS = 4, 4, 8, 16
GROUP = 8
TOK = 512
COLS = 256
STATE = 256
SLICE = STATE // GROUP
ROWS = 256
TILE = 256
CHUNK = 128
NCHUNK = TOK // CHUNK
EXP2_SCALE = HEAD**-0.5 * 1.4426950408889634
F32 = jnp.float32
BF16 = jnp.bfloat16


def device(x, y, z, c):
    return ((z // ZLO) * XS + x, (z % ZLO) * GROUP + y * 2 + c)


def nt(a, b):
    return lax.dot_general(a, b, (((1,), (1,)), ((), ())), preferred_element_type=F32)


def nn(a, b):
    return lax.dot_general(a, b, (((1,), (0,)), ((), ())), preferred_element_type=F32)


def remote(src, dst, send, recv, target):
    return pltpu.make_async_remote_copy(
        src_ref=src, dst_ref=dst, send_sem=send, recv_sem=recv, device_id=target, device_id_type=MESH
    )


def kernel(
    q_hbm, k_hbm, v_hbm, sq_hbm, g_hbm, w_hbm, o_ref,
    q, k, v, sq, vt, kprev, vprev, gates, asend, arecv, tsend, trecv, ktsend, ktrecv,
    enter, gain, csend, mem, wbuf, top, total, acc, xatt, zsend, zrecv, own,
    lsem, wl_sem, as_sem, ar_sem, gs_sem, gr_sem, kvs_sem, kvr_sem, ws_sem, wr_sem,
    bs_sem, br_sem, bks_sem, bkr_sem, cs_sem, cr_sem, xs_sem, xr_sem, zs_sem, zr_sem, ready,
):
    dp = lax.axis_index("dp")
    seq = lax.axis_index("seq")
    x = dp % XS
    zlo = seq // GROUP
    z = (dp // XS) * ZLO + zlo
    r = seq % GROUP
    y = r // 2
    c = r % 2
    partner = ((dp + XS) % (2 * XS), seq)

    def in_group(j):
        other = (r + j) % GROUP
        return other, (dp, zlo * GROUP + other)

    def on_x(j):
        other = (x + j) % XS
        return other, ((dp // XS) * XS + other, seq)

    last_of_plane = (r == GROUP - 1) & (zlo < ZLO - 1)
    first_of_plane = (r == 0) & (zlo > 0)

    barrier = pltpu.get_barrier_semaphore()
    greeted = [in_group(j)[1] for j in range(1, GROUP)]
    greeted += [on_x(j)[1] for j in range(1, XS)]
    greeted += [device(x, y, (z + d) % ZS, c) for d in (1, 2, 3, 4, 12, 13, 14, 15)]
    for target in greeted:
        pl.semaphore_signal(barrier, inc=1, device_id=target, device_id_type=MESH)

    @pl.when(last_of_plane)
    def _():
        pl.semaphore_signal(barrier, inc=1, device_id=(dp, seq + 1), device_id_type=MESH)

    @pl.when(first_of_plane)
    def _():
        pl.semaphore_signal(barrier, inc=1, device_id=(dp, seq - 1), device_id_type=MESH)

    loads = [
        pltpu.make_async_copy(src, dst, lsem.at[i])
        for i, (src, dst) in enumerate(
            ((k_hbm, k), (sq_hbm, sq), (v_hbm, v), (g_hbm, gates.at[r]), (q_hbm, q))
        )
    ]
    for copy in loads:
        copy.start()
    own_rows = pl.ds(pl.multiple_of(dp * ROWS, ROWS), ROWS)
    partner_rows = pl.ds(pl.multiple_of(partner[0] * ROWS, ROWS), ROWS)
    own_cols = pl.ds(pl.multiple_of(x * COLS, COLS), COLS)
    w_loads = [
        pltpu.make_async_copy(w_hbm.at[own_rows], wbuf.at[0, :, own_cols], wl_sem.at[0]),
        pltpu.make_async_copy(w_hbm.at[partner_rows], wbuf.at[1, :, own_cols], wl_sem.at[1]),
    ]
    for copy in w_loads:
        copy.start()

    loads[0].wait()
    loads[1].wait()
    loads[2].wait()
    loads[3].wait()
    vt[...] = v[...].T
    keep_own = jax.nn.sigmoid(gates[r])
    for h in range(2):
        cols = slice(h * HEAD, (h + 1) * HEAD)
        scores = nt(k[:, cols], sq[:, cols])
        highest = jnp.max(scores, axis=0, keepdims=True)
        weights = jnp.exp2(scores * EXP2_SCALE - highest * EXP2_SCALE)
        sums = jnp.sum(weights, axis=0, keepdims=True)
        update = nn(vt[cols, :], weights.astype(BF16)) / sums
        asend[:, cols] = ((1.0 - keep_own[:, cols]) * update.T).astype(BF16)

    pl.semaphore_wait(
        barrier,
        len(greeted) + last_of_plane.astype(jnp.int32) + first_of_plane.astype(jnp.int32),
    )
    pl.semaphore_signal(
        ready, inc=1, device_id=device(x, y, (z + ZS - 4) % ZS, c), device_id_type=MESH
    )

    slice_rows = pl.ds(pl.multiple_of(r * SLICE, SLICE), SLICE)
    a_copies, g_copies, w_copies = [], [], []
    for j in range(1, GROUP):
        other, target = in_group(j)
        rows = pl.ds(pl.multiple_of(other * SLICE, SLICE), SLICE)
        a_copies.append(
            remote(asend.at[rows], arecv.at[r], as_sem.at[j], ar_sem.at[j], target)
        )
        g_copies.append(remote(g_hbm, gates.at[r], gs_sem.at[j], gr_sem.at[j], target))
        g_copies[-1].start()
        a_copies[-1].start()
    for j in (1, 3, 2):
        other, target = on_x(j)
        base = (dp // XS) * XS
        for part, owner in ((0, base + other), (1, (base + XS) % (2 * XS) + other)):
            rows = pl.ds(pl.multiple_of(owner * ROWS, ROWS), ROWS)
            w_copies.append(
                remote(
                    w_hbm.at[rows], wbuf.at[part, :, own_cols],
                    ws_sem.at[j, part], wr_sem.at[j, part], target,
                )
            )
            w_copies[-1].start()

    kv_copies = [
        remote(src, dst, kvs_sem.at[i], kvr_sem.at[i], (dp, jnp.minimum(seq + 1, 63)))
        for i, (src, dst) in enumerate(((k_hbm, kprev), (v_hbm, vprev)))
    ]

    @pl.when(seq < 63)
    def _():
        for copy in kv_copies:
            copy.start()

    arecv[r] = asend[slice_rows, :]

    loads[4].wait()

    def token_part(keys, values_t, h, t, low, high, later, first):
        cols = slice(h * HEAD, (h + 1) * HEAD)
        toks = slice(t * TILE, (t + 1) * TILE)
        scores = nt(keys[low:high, cols], q[toks, cols])
        key_at = lax.broadcasted_iota(jnp.int32, scores.shape, 0) + low
        tok_at = lax.broadcasted_iota(jnp.int32, scores.shape, 1) + t * TILE
        seen = key_at > tok_at if later else key_at <= tok_at
        scores = jnp.where(seen, scores * EXP2_SCALE, -1e30)
        highest = jnp.max(scores, axis=0, keepdims=True)
        if not first:
            before = top[h, :, toks]
            highest = jnp.maximum(highest, before)
            fade = jnp.exp2(before - highest)
        weights = jnp.exp2(scores - highest)
        sums = jnp.sum(weights, axis=0, keepdims=True)
        summed = nn(values_t[cols, low:high], weights.astype(BF16))
        top[h, :, toks] = highest
        if first:
            total[h, :, toks] = sums
            acc[cols, toks] = summed
        else:
            total[h, :, toks] = fade * total[h, :, toks] + sums
            acc[cols, toks] = fade * acc[cols, toks] + summed

    for h in range(2):
        for t in range(TOK // TILE):
            token_part(k, vt, h, t, 0, (t + 1) * TILE, False, True)

    for copy in g_copies:
        copy.wait_recv()
    for copy in a_copies:
        copy.wait_recv()
    run_v = jnp.zeros((SLICE, COLS), F32)
    run_k = jnp.ones((1, COLS), F32)
    inner = []
    for b in range(GROUP):
        inner.append((run_k, run_v))
        keep = jax.nn.sigmoid(gates[b])
        run_v = keep * run_v + arecv[b].astype(F32)
        run_k = keep * run_k
    tsend[...] = run_v.astype(BF16)
    ktsend[...] = run_k

    def to_plane(d):
        target = (dp, jnp.minimum(zlo + d, ZLO - 1) * GROUP + r)
        return (
            remote(tsend, trecv.at[d - 1], bs_sem.at[d - 1], br_sem.at[d - 1], target),
            remote(ktsend, ktrecv.at[d - 1], bks_sem.at[d - 1], bkr_sem.at[d - 1], target),
        )

    b_copies = [to_plane(d) for d in range(1, ZLO)]
    for d in range(1, ZLO):
        if d == 5:
            pl.semaphore_wait(ready, 1)

        @pl.when(zlo + d < ZLO)
        def _():
            for copy in b_copies[d - 1]:
                copy.start()

    enter[...] = jnp.zeros_like(enter)
    gain[...] = jnp.ones_like(gain)
    for d in range(1, ZLO):

        @pl.when(zlo >= d)
        def _():
            for copy in b_copies[d - 1]:
                copy.wait_recv()
            enter[...] += gain[...] * trecv[d - 1].astype(F32)
            gain[...] = gain[...] * ktrecv[d - 1]

    for b in range(GROUP):
        inner_k, inner_v = inner[b]
        csend[b] = (inner_k * enter[...] + inner_v).astype(BF16)
    c_copies = []
    for j in range(1, GROUP):
        other, target = in_group(j)
        c_copies.append(
            remote(csend.at[other], mem.at[slice_rows], cs_sem.at[j], cr_sem.at[j], target)
        )
        c_copies[-1].start()
    mem[slice_rows, :] = csend[r]

    @pl.when(seq > 0)
    def _():
        for copy in kv_copies:
            copy.wait_recv()
        vt[...] = vprev[...].T
        for h in range(2):
            for t in range(TOK // TILE):
                token_part(kprev, vt, h, t, t * TILE, TOK, True, False)

    for copy in c_copies:
        copy.wait_recv()
    mem_t = mem[...].T
    x_rows = pl.ds(pl.multiple_of(x * COLS, COLS), COLS)
    x_copies = []
    for n in range(NCHUNK):
        toks = slice(n * CHUNK, (n + 1) * CHUNK)
        for h in range(2):
            cols = slice(h * HEAD, (h + 1) * HEAD)
            scores = nt(mem[:, cols], q[toks, cols]) * EXP2_SCALE
            before = top[h, :, toks]
            highest = jnp.maximum(jnp.max(scores, axis=0, keepdims=True), before)
            fade = jnp.exp2(before - highest)
            weights = jnp.exp2(scores - highest)
            sums = fade * total[h, :, toks] + jnp.sum(weights, axis=0, keepdims=True)
            summed = fade * acc[cols, toks] + nn(mem_t[cols, :], weights.astype(BF16))
            xatt[n, pl.ds(pl.multiple_of(x * COLS + h * HEAD, HEAD), HEAD), :] = (
                summed / sums
            ).astype(BF16)
        sent = []
        for j in (1, 3, 2):
            _, target = on_x(j)
            sent.append(
                remote(
                    xatt.at[n, x_rows], xatt.at[n, x_rows], xs_sem.at[n, j], xr_sem.at[n, j], target
                )
            )
            sent[-1].start()
        x_copies.append(sent)

    for copy in w_loads:
        copy.wait()
    for copy in w_copies:
        copy.wait_recv()
    z_copies = []
    for n in range(NCHUNK):
        for copy in x_copies[n]:
            copy.wait_recv()
        zsend[n] = nn(wbuf[1], xatt[n]).astype(BF16)
        z_copies.append(remote(zsend.at[n], zrecv.at[n], zs_sem.at[n], zr_sem.at[n], partner))
        z_copies[-1].start()
    for n in range(NCHUNK):
        own[n] = nn(wbuf[0], xatt[n])
    for n in range(NCHUNK):
        z_copies[n].wait_recv()
        o_ref[:, n * CHUNK : (n + 1) * CHUNK] = (own[n] + zrecv[n].astype(F32)).astype(BF16)

    for copy in g_copies + a_copies + w_copies + c_copies + z_copies:
        copy.wait_send()
    for sent in x_copies:
        for copy in sent:
            copy.wait_send()

    @pl.when(seq < 63)
    def _():
        for copy in kv_copies:
            copy.wait_send()

    for d in range(1, ZLO):

        @pl.when(zlo + d < ZLO)
        def _():
            for copy in b_copies[d - 1]:
                copy.wait_send()


def body(queries, key_rows, value_rows, slot_queries, gate_logit, out_weight):
    dma = pltpu.SemaphoreType.DMA
    vmem = pltpu.VMEM
    return pl.pallas_call(
        kernel,
        out_shape=jax.ShapeDtypeStruct((ROWS, TOK), BF16),
        in_specs=[pl.BlockSpec(memory_space=pl.ANY)] * 6,
        out_specs=pl.BlockSpec(memory_space=pltpu.VMEM),
        scratch_shapes=[
            vmem((TOK, COLS), BF16),
            vmem((TOK, COLS), BF16),
            vmem((TOK, COLS), BF16),
            vmem((STATE, COLS), BF16),
            vmem((COLS, TOK), BF16),
            vmem((TOK, COLS), BF16),
            vmem((TOK, COLS), BF16),
            vmem((GROUP, 1, COLS), F32),
            vmem((STATE, COLS), BF16),
            vmem((GROUP, SLICE, COLS), BF16),
            vmem((SLICE, COLS), BF16),
            vmem((ZLO - 1, SLICE, COLS), BF16),
            vmem((1, COLS), F32),
            vmem((ZLO - 1, 1, COLS), F32),
            vmem((SLICE, COLS), F32),
            vmem((1, COLS), F32),
            vmem((GROUP, SLICE, COLS), BF16),
            vmem((STATE, COLS), BF16),
            vmem((2, ROWS, XS * COLS), BF16),
            vmem((2, 1, TOK), F32),
            vmem((2, 1, TOK), F32),
            vmem((COLS, TOK), F32),
            vmem((NCHUNK, XS * COLS, CHUNK), BF16),
            vmem((NCHUNK, ROWS, CHUNK), BF16),
            vmem((NCHUNK, ROWS, CHUNK), BF16),
            vmem((NCHUNK, ROWS, CHUNK), F32),
            dma((5,)),
            dma((2,)),
            dma((GROUP,)),
            dma((GROUP,)),
            dma((GROUP,)),
            dma((GROUP,)),
            dma((2,)),
            dma((2,)),
            dma((XS, 2)),
            dma((XS, 2)),
            dma((ZLO - 1,)),
            dma((ZLO - 1,)),
            dma((ZLO - 1,)),
            dma((ZLO - 1,)),
            dma((GROUP,)),
            dma((GROUP,)),
            dma((NCHUNK, XS)),
            dma((NCHUNK, XS)),
            dma((NCHUNK,)),
            dma((NCHUNK,)),
            pltpu.SemaphoreType.REGULAR,
        ],
        compiler_params=pltpu.CompilerParams(collective_id=0, has_side_effects=True),
    )(queries, key_rows, value_rows, slot_queries, gate_logit, out_weight)


def solution(mesh):
    in_specs = (
        P("seq", "dp"),
        P("seq", "dp"),
        P("seq", "dp"),
        P(None, "dp"),
        P("seq", "dp"),
        P(None, "dp"),
    )
    return jax.shard_map(
        body, mesh=mesh, in_specs=in_specs, out_specs=P("dp", "seq"), check_vma=False
    )
```

```python
import functools

import jax
import jax.numpy as jnp
from jax import lax
from jax.experimental import pallas as pl
from jax.experimental.pallas import tpu as pltpu
from jax.sharding import PartitionSpec as P

HEAD = 128
MESH = pl.DeviceIdType.MESH
XS, YS, ZLO, ZS = 4, 4, 8, 16
GROUP = 8
TOK = 512
COLS = 256
STATE = 256
SLICE = STATE // GROUP
EXTRA = 16
ROWS = 256
TILE = 256
CHUNK = 128
NCHUNK = TOK // CHUNK
EXP2_SCALE = HEAD**-0.5 * 1.4426950408889634
F32 = jnp.float32
BF16 = jnp.bfloat16


def device(x, y, z, c):
    return ((z // ZLO) * XS + x, (z % ZLO) * GROUP + y * 2 + c)


def nt(a, b):
    return lax.dot_general(a, b, (((1,), (1,)), ((), ())), preferred_element_type=F32)


def nn(a, b):
    return lax.dot_general(a, b, (((1,), (0,)), ((), ())), preferred_element_type=F32)


def in_parts(rate):
    high = rate.astype(BF16)
    rest = rate - high.astype(F32)
    middle = rest.astype(BF16)
    low = (rest - middle.astype(F32)).astype(BF16)
    row = lax.broadcasted_iota(jnp.int32, (EXTRA, COLS), 0)
    wide = [jnp.broadcast_to(part.astype(F32), (EXTRA, COLS)) for part in (high, middle, low)]
    return jnp.where(row == 0, wide[0], jnp.where(row == 1, wide[1], wide[2])).astype(BF16)


def from_parts(rows):
    wide = rows.astype(F32)
    return (wide[0:1] + wide[1:2]) + wide[2:3]


def remote(src, dst, send, recv, target):
    return pltpu.make_async_remote_copy(
        src_ref=src, dst_ref=dst, send_sem=send, recv_sem=recv, device_id=target, device_id_type=MESH
    )


def kernel(
    q_hbm, k_hbm, v_hbm, sq_hbm, g_hbm, w_hbm, o_ref,
    q, k, v, sq, vt, kprev, vprev, gate, asend, arecv, tsend, trecv, ktsend, ktrecv,
    enter, gain, csend, mem, wbuf, top, total, acc, xatt, zsend, zrecv, own,
    lsem, wl_sem, as_sem, ar_sem, kvs_sem, kvr_sem, ws_sem, wr_sem,
    bs_sem, br_sem, bks_sem, bkr_sem, cs_sem, cr_sem, xs_sem, xr_sem, zs_sem, zr_sem, ready,
):
    dp = lax.axis_index("dp")
    seq = lax.axis_index("seq")
    x = dp % XS
    zlo = seq // GROUP
    z = (dp // XS) * ZLO + zlo
    r = seq % GROUP
    y = r // 2
    c = r % 2
    partner = ((dp + XS) % (2 * XS), seq)

    def in_group(j):
        other = (r + j) % GROUP
        return other, (dp, zlo * GROUP + other)

    def on_x(j):
        other = (x + j) % XS
        return other, ((dp // XS) * XS + other, seq)

    last_of_plane = (r == GROUP - 1) & (zlo < ZLO - 1)
    first_of_plane = (r == 0) & (zlo > 0)

    loads = [
        pltpu.make_async_copy(src, dst, lsem.at[i])
        for i, (src, dst) in enumerate(
            ((k_hbm, k), (sq_hbm, sq), (v_hbm, v), (g_hbm, gate), (q_hbm, q))
        )
    ]
    for copy in loads:
        copy.start()

    barrier = pltpu.get_barrier_semaphore()
    greeted = [in_group(j)[1] for j in range(1, GROUP)]
    greeted += [on_x(j)[1] for j in range(1, XS)]
    greeted += [device(x, y, (z + d) % ZS, c) for d in (1, 2, 3, 4, 12, 13, 14, 15)]
    for target in greeted:
        pl.semaphore_signal(barrier, inc=1, device_id=target, device_id_type=MESH)

    @pl.when(last_of_plane)
    def _():
        pl.semaphore_signal(barrier, inc=1, device_id=(dp, seq + 1), device_id_type=MESH)

    @pl.when(first_of_plane)
    def _():
        pl.semaphore_signal(barrier, inc=1, device_id=(dp, seq - 1), device_id_type=MESH)

    own_rows = pl.ds(pl.multiple_of(dp * ROWS, ROWS), ROWS)
    partner_rows = pl.ds(pl.multiple_of(partner[0] * ROWS, ROWS), ROWS)
    own_cols = pl.ds(pl.multiple_of(x * COLS, COLS), COLS)
    w_loads = [
        pltpu.make_async_copy(w_hbm.at[own_rows], wbuf.at[0, :, own_cols], wl_sem.at[0]),
        pltpu.make_async_copy(w_hbm.at[partner_rows], wbuf.at[1, :, own_cols], wl_sem.at[1]),
    ]
    for copy in w_loads:
        copy.start()

    loads[0].wait()
    loads[1].wait()
    loads[2].wait()
    loads[3].wait()
    vt[...] = v[...].T
    keep_own = jax.nn.sigmoid(gate[...])
    parts = in_parts(keep_own)
    for h in range(2):
        cols = slice(h * HEAD, (h + 1) * HEAD)
        scores = nt(k[:, cols], sq[:, cols])
        highest = jnp.max(scores, axis=0, keepdims=True)
        weights = jnp.exp2(scores * EXP2_SCALE - highest * EXP2_SCALE)
        sums = jnp.sum(weights, axis=0, keepdims=True)
        update = nn(vt[cols, :], weights.astype(BF16)) / sums
        kept = ((1.0 - keep_own[:, cols]) * update.T).astype(BF16)
        for b in range(GROUP):
            asend[b, :SLICE, cols] = kept[b * SLICE : (b + 1) * SLICE]
    for b in range(GROUP):
        asend[b, SLICE:, :] = parts

    pl.semaphore_wait(
        barrier,
        len(greeted) + last_of_plane.astype(jnp.int32) + first_of_plane.astype(jnp.int32),
    )
    pl.semaphore_signal(
        ready, inc=1, device_id=device(x, y, (z + ZS - 4) % ZS, c), device_id_type=MESH
    )

    slice_rows = pl.ds(pl.multiple_of(r * SLICE, SLICE), SLICE)
    a_copies, w_copies = [], []
    for j in range(1, GROUP):
        other, target = in_group(j)
        a_copies.append(
            remote(asend.at[other], arecv.at[r], as_sem.at[j], ar_sem.at[j], target)
        )
        a_copies[-1].start()
    for j in (1, 3, 2):
        other, target = on_x(j)
        base = (dp // XS) * XS
        for part, owner in ((0, base + other), (1, (base + XS) % (2 * XS) + other)):
            rows = pl.ds(pl.multiple_of(owner * ROWS, ROWS), ROWS)
            w_copies.append(
                remote(
                    w_hbm.at[rows], wbuf.at[part, :, own_cols],
                    ws_sem.at[j, part], wr_sem.at[j, part], target,
                )
            )
            w_copies[-1].start()

    kv_copies = [
        remote(src, dst, kvs_sem.at[i], kvr_sem.at[i], (dp, jnp.minimum(seq + 1, 63)))
        for i, (src, dst) in enumerate(((k_hbm, kprev), (v_hbm, vprev)))
    ]

    @pl.when(seq < 63)
    def _():
        for copy in kv_copies:
            copy.start()

    arecv[r] = asend[r]

    loads[4].wait()

    def token_part(keys, values_t, h, t, low, high, later, first):
        cols = slice(h * HEAD, (h + 1) * HEAD)
        toks = slice(t * TILE, (t + 1) * TILE)
        scores = nt(keys[low:high, cols], q[toks, cols])
        key_at = lax.broadcasted_iota(jnp.int32, scores.shape, 0) + low
        tok_at = lax.broadcasted_iota(jnp.int32, scores.shape, 1) + t * TILE
        seen = key_at > tok_at if later else key_at <= tok_at
        scores = jnp.where(seen, scores * EXP2_SCALE, -1e30)
        highest = jnp.max(scores, axis=0, keepdims=True)
        if not first:
            before = top[h, :, toks]
            highest = jnp.maximum(highest, before)
            fade = jnp.exp2(before - highest)
        weights = jnp.exp2(scores - highest)
        sums = jnp.sum(weights, axis=0, keepdims=True)
        summed = nn(values_t[cols, low:high], weights.astype(BF16))
        top[h, :, toks] = highest
        if first:
            total[h, :, toks] = sums
            acc[cols, toks] = summed
        else:
            total[h, :, toks] = fade * total[h, :, toks] + sums
            acc[cols, toks] = fade * acc[cols, toks] + summed

    for h in range(2):
        for t in range(TOK // TILE):
            token_part(k, vt, h, t, 0, (t + 1) * TILE, False, True)

    for copy in a_copies:
        copy.wait_recv()
    run_v = jnp.zeros((SLICE, COLS), F32)
    run_k = jnp.ones((1, COLS), F32)
    inner = []
    for b in range(GROUP):
        inner.append((run_k, run_v))
        keep = from_parts(arecv[b, SLICE:, :])
        run_v = keep * run_v + arecv[b, :SLICE, :].astype(F32)
        run_k = keep * run_k
    tsend[...] = run_v.astype(BF16)
    ktsend[...] = run_k

    def to_plane(d):
        target = (dp, jnp.minimum(zlo + d, ZLO - 1) * GROUP + r)
        return (
            remote(tsend, trecv.at[d - 1], bs_sem.at[d - 1], br_sem.at[d - 1], target),
            remote(ktsend, ktrecv.at[d - 1], bks_sem.at[d - 1], bkr_sem.at[d - 1], target),
        )

    b_copies = [to_plane(d) for d in range(1, ZLO)]
    for d in range(1, ZLO):
        if d == 5:
            pl.semaphore_wait(ready, 1)

        @pl.when(zlo + d < ZLO)
        def _():
            for copy in b_copies[d - 1]:
                copy.start()

    enter[...] = jnp.zeros_like(enter)
    gain[...] = jnp.ones_like(gain)
    for d in range(1, ZLO):

        @pl.when(zlo >= d)
        def _():
            for copy in b_copies[d - 1]:
                copy.wait_recv()
            enter[...] += gain[...] * trecv[d - 1].astype(F32)
            gain[...] = gain[...] * ktrecv[d - 1]

    for b in range(GROUP):
        inner_k, inner_v = inner[b]
        csend[b] = (inner_k * enter[...] + inner_v).astype(BF16)
    c_copies = []
    for j in range(1, GROUP):
        other, target = in_group(j)
        c_copies.append(
            remote(csend.at[other], mem.at[slice_rows], cs_sem.at[j], cr_sem.at[j], target)
        )
        c_copies[-1].start()
    mem[slice_rows, :] = csend[r]

    @pl.when(seq > 0)
    def _():
        for copy in kv_copies:
            copy.wait_recv()
        vt[...] = vprev[...].T
        for h in range(2):
            for t in range(TOK // TILE):
                token_part(kprev, vt, h, t, t * TILE, TOK, True, False)

    for copy in c_copies:
        copy.wait_recv()
    mem_t = mem[...].T
    x_rows = pl.ds(pl.multiple_of(x * COLS, COLS), COLS)
    x_copies = []
    for n in range(NCHUNK):
        toks = slice(n * CHUNK, (n + 1) * CHUNK)
        for h in range(2):
            cols = slice(h * HEAD, (h + 1) * HEAD)
            scores = nt(mem[:, cols], q[toks, cols]) * EXP2_SCALE
            before = top[h, :, toks]
            highest = jnp.maximum(jnp.max(scores, axis=0, keepdims=True), before)
            fade = jnp.exp2(before - highest)
            weights = jnp.exp2(scores - highest)
            sums = fade * total[h, :, toks] + jnp.sum(weights, axis=0, keepdims=True)
            summed = fade * acc[cols, toks] + nn(mem_t[cols, :], weights.astype(BF16))
            xatt[n, pl.ds(pl.multiple_of(x * COLS + h * HEAD, HEAD), HEAD), :] = (
                summed / sums
            ).astype(BF16)
        sent = []
        for j in (1, 3, 2):
            _, target = on_x(j)
            sent.append(
                remote(
                    xatt.at[n, x_rows], xatt.at[n, x_rows], xs_sem.at[n, j], xr_sem.at[n, j], target
                )
            )
            sent[-1].start()
        x_copies.append(sent)

    for copy in w_loads:
        copy.wait()
    for copy in w_copies:
        copy.wait_recv()
    z_copies = []
    for n in range(NCHUNK):
        for copy in x_copies[n]:
            copy.wait_recv()
        zsend[n] = nn(wbuf[1], xatt[n]).astype(BF16)
        z_copies.append(remote(zsend.at[n], zrecv.at[n], zs_sem.at[n], zr_sem.at[n], partner))
        z_copies[-1].start()
    for n in range(NCHUNK):
        own[n] = nn(wbuf[0], xatt[n])
    for n in range(NCHUNK):
        z_copies[n].wait_recv()
        o_ref[:, n * CHUNK : (n + 1) * CHUNK] = (own[n] + zrecv[n].astype(F32)).astype(BF16)

    for copy in a_copies + w_copies + c_copies + z_copies:
        copy.wait_send()
    for sent in x_copies:
        for copy in sent:
            copy.wait_send()

    @pl.when(seq < 63)
    def _():
        for copy in kv_copies:
            copy.wait_send()

    for d in range(1, ZLO):

        @pl.when(zlo + d < ZLO)
        def _():
            for copy in b_copies[d - 1]:
                copy.wait_send()


def body(queries, key_rows, value_rows, slot_queries, gate_logit, out_weight):
    dma = pltpu.SemaphoreType.DMA
    vmem = pltpu.VMEM
    return pl.pallas_call(
        kernel,
        out_shape=pltpu.VMEM((ROWS, TOK), BF16),
        in_specs=[pl.BlockSpec(memory_space=pl.ANY)] * 6,
        out_specs=pl.BlockSpec(memory_space=pltpu.VMEM),
        scratch_shapes=[
            vmem((TOK, COLS), BF16),
            vmem((TOK, COLS), BF16),
            vmem((TOK, COLS), BF16),
            vmem((STATE, COLS), BF16),
            vmem((COLS, TOK), BF16),
            vmem((TOK, COLS), BF16),
            vmem((TOK, COLS), BF16),
            vmem((1, COLS), F32),
            vmem((GROUP, SLICE + EXTRA, COLS), BF16),
            vmem((GROUP, SLICE + EXTRA, COLS), BF16),
            vmem((SLICE, COLS), BF16),
            vmem((ZLO - 1, SLICE, COLS), BF16),
            vmem((1, COLS), F32),
            vmem((ZLO - 1, 1, COLS), F32),
            vmem((SLICE, COLS), F32),
            vmem((1, COLS), F32),
            vmem((GROUP, SLICE, COLS), BF16),
            vmem((STATE, COLS), BF16),
            vmem((2, ROWS, XS * COLS), BF16),
            vmem((2, 1, TOK), F32),
            vmem((2, 1, TOK), F32),
            vmem((COLS, TOK), F32),
            vmem((NCHUNK, XS * COLS, CHUNK), BF16),
            vmem((NCHUNK, ROWS, CHUNK), BF16),
            vmem((NCHUNK, ROWS, CHUNK), BF16),
            vmem((NCHUNK, ROWS, CHUNK), F32),
            dma((5,)),
            dma((2,)),
            dma((GROUP,)),
            dma((GROUP,)),
            dma((2,)),
            dma((2,)),
            dma((XS, 2)),
            dma((XS, 2)),
            dma((ZLO - 1,)),
            dma((ZLO - 1,)),
            dma((ZLO - 1,)),
            dma((ZLO - 1,)),
            dma((GROUP,)),
            dma((GROUP,)),
            dma((NCHUNK, XS)),
            dma((NCHUNK, XS)),
            dma((NCHUNK,)),
            dma((NCHUNK,)),
            pltpu.SemaphoreType.REGULAR,
        ],
        compiler_params=pltpu.CompilerParams(collective_id=0, has_side_effects=True),
    )(queries, key_rows, value_rows, slot_queries, gate_logit, out_weight)


def solution(mesh):
    in_specs = (
        P("seq", "dp"),
        P("seq", "dp"),
        P("seq", "dp"),
        P(None, "dp"),
        P("seq", "dp"),
        P(None, "dp"),
    )
    return jax.shard_map(
        body, mesh=mesh, in_specs=in_specs, out_specs=P("dp", "seq"), check_vma=False
    )
```

```python
import functools

import jax
import jax.numpy as jnp
from jax import lax
from jax.experimental import pallas as pl
from jax.experimental.pallas import tpu as pltpu
from jax.sharding import PartitionSpec as P

HEAD = 128
MESH = pl.DeviceIdType.MESH
XS, YS, ZLO, ZS = 4, 4, 8, 16
GROUP = 8
TOK = 512
COLS = 256
STATE = 256
SLICE = STATE // GROUP
EXTRA = 16
ROWS = 256
TILE = 256
CHUNK = 128
NCHUNK = TOK // CHUNK
EXP2_SCALE = HEAD**-0.5 * 1.4426950408889634
F32 = jnp.float32
BF16 = jnp.bfloat16


def device(x, y, z, c):
    return ((z // ZLO) * XS + x, (z % ZLO) * GROUP + y * 2 + c)


def nt(a, b):
    return lax.dot_general(a, b, (((1,), (1,)), ((), ())), preferred_element_type=F32)


def nn(a, b):
    return lax.dot_general(a, b, (((1,), (0,)), ((), ())), preferred_element_type=F32)


def in_parts(rate):
    high = rate.astype(BF16)
    rest = rate - high.astype(F32)
    middle = rest.astype(BF16)
    low = (rest - middle.astype(F32)).astype(BF16)
    row = lax.broadcasted_iota(jnp.int32, (EXTRA, COLS), 0)
    wide = [jnp.broadcast_to(part.astype(F32), (EXTRA, COLS)) for part in (high, middle, low)]
    return jnp.where(row == 0, wide[0], jnp.where(row == 1, wide[1], wide[2])).astype(BF16)


def from_parts(rows):
    wide = rows.astype(F32)
    return (wide[0:1] + wide[1:2]) + wide[2:3]


def remote(src, dst, send, recv, target):
    return pltpu.make_async_remote_copy(
        src_ref=src, dst_ref=dst, send_sem=send, recv_sem=recv, device_id=target, device_id_type=MESH
    )


def kernel(
    q_hbm, k_hbm, v_hbm, sq_hbm, g_hbm, w_hbm, o_ref,
    q, k, v, sq, vt, kprev, vprev, gate, asend, arecv, tsend, trecv, ktsend, ktrecv,
    enter, gain, csend, mem, wbuf, top, total, acc, xatt, zsend, zrecv, own,
    lsem, wl_sem, as_sem, ar_sem, kvs_sem, kvr_sem, ws_sem, wr_sem,
    bs_sem, br_sem, bks_sem, bkr_sem, cs_sem, cr_sem, xs_sem, xr_sem, zs_sem, zr_sem, ready,
):
    dp = lax.axis_index("dp")
    seq = lax.axis_index("seq")
    x = dp % XS
    zlo = seq // GROUP
    z = (dp // XS) * ZLO + zlo
    r = seq % GROUP
    y = r // 2
    c = r % 2
    partner = ((dp + XS) % (2 * XS), seq)

    def in_group(j):
        other = (r + j) % GROUP
        return other, (dp, zlo * GROUP + other)

    def on_x(j):
        other = (x + j) % XS
        return other, ((dp // XS) * XS + other, seq)

    last_of_plane = (r == GROUP - 1) & (zlo < ZLO - 1)
    first_of_plane = (r == 0) & (zlo > 0)

    loads = [
        pltpu.make_async_copy(src, dst, lsem.at[i])
        for i, (src, dst) in enumerate(
            ((k_hbm, k), (sq_hbm, sq), (v_hbm, v), (g_hbm, gate), (q_hbm, q))
        )
    ]
    for copy in loads:
        copy.start()

    barrier = pltpu.get_barrier_semaphore()
    greeted = [in_group(j)[1] for j in range(1, GROUP)]
    greeted += [on_x(j)[1] for j in range(1, XS)]
    greeted += [device(x, y, (z + d) % ZS, c) for d in (1, 15)]
    for target in greeted:
        pl.semaphore_signal(barrier, inc=1, device_id=target, device_id_type=MESH)

    @pl.when(last_of_plane)
    def _():
        pl.semaphore_signal(barrier, inc=1, device_id=(dp, seq + 1), device_id_type=MESH)

    @pl.when(first_of_plane)
    def _():
        pl.semaphore_signal(barrier, inc=1, device_id=(dp, seq - 1), device_id_type=MESH)

    own_rows = pl.ds(pl.multiple_of(dp * ROWS, ROWS), ROWS)
    partner_rows = pl.ds(pl.multiple_of(partner[0] * ROWS, ROWS), ROWS)
    own_cols = pl.ds(pl.multiple_of(x * COLS, COLS), COLS)
    w_loads = [
        pltpu.make_async_copy(w_hbm.at[own_rows], wbuf.at[0, :, own_cols], wl_sem.at[0]),
        pltpu.make_async_copy(w_hbm.at[partner_rows], wbuf.at[1, :, own_cols], wl_sem.at[1]),
    ]
    for copy in w_loads:
        copy.start()

    loads[0].wait()
    loads[1].wait()
    loads[2].wait()
    loads[3].wait()
    vt[...] = v[...].T
    keep_own = jax.nn.sigmoid(gate[...])
    parts = in_parts(keep_own)
    for h in range(2):
        cols = slice(h * HEAD, (h + 1) * HEAD)
        scores = nt(k[:, cols], sq[:, cols])
        highest = jnp.max(scores, axis=0, keepdims=True)
        weights = jnp.exp2(scores * EXP2_SCALE - highest * EXP2_SCALE)
        sums = jnp.sum(weights, axis=0, keepdims=True)
        update = nn(vt[cols, :], weights.astype(BF16)) / sums
        kept = ((1.0 - keep_own[:, cols]) * update.T).astype(BF16)
        for b in range(GROUP):
            asend[b, :SLICE, cols] = kept[b * SLICE : (b + 1) * SLICE]
    for b in range(GROUP):
        asend[b, SLICE:, :] = parts

    pl.semaphore_wait(
        barrier,
        len(greeted) + last_of_plane.astype(jnp.int32) + first_of_plane.astype(jnp.int32),
    )

    def tell(n):
        for d in (1 << n, ZS - (1 << n)):
            pl.semaphore_signal(
                ready.at[n], inc=1, device_id=device(x, y, (z + d) % ZS, c), device_id_type=MESH
            )

    tell(0)
    slice_rows = pl.ds(pl.multiple_of(r * SLICE, SLICE), SLICE)
    a_copies, w_copies = [], []
    for j in range(1, GROUP):
        other, target = in_group(j)
        a_copies.append(
            remote(asend.at[other], arecv.at[r], as_sem.at[j], ar_sem.at[j], target)
        )
        a_copies[-1].start()
    for j in (1, 3, 2):
        other, target = on_x(j)
        base = (dp // XS) * XS
        for part, owner in ((0, base + other), (1, (base + XS) % (2 * XS) + other)):
            rows = pl.ds(pl.multiple_of(owner * ROWS, ROWS), ROWS)
            w_copies.append(
                remote(
                    w_hbm.at[rows], wbuf.at[part, :, own_cols],
                    ws_sem.at[j, part], wr_sem.at[j, part], target,
                )
            )
            w_copies[-1].start()

    kv_copies = [
        remote(src, dst, kvs_sem.at[i], kvr_sem.at[i], (dp, jnp.minimum(seq + 1, 63)))
        for i, (src, dst) in enumerate(((k_hbm, kprev), (v_hbm, vprev)))
    ]

    @pl.when(seq < 63)
    def _():
        for copy in kv_copies:
            copy.start()

    arecv[r] = asend[r]

    pl.semaphore_wait(ready.at[0], 2)
    tell(1)

    loads[4].wait()

    def token_part(keys, values_t, h, t, low, high, later, first):
        cols = slice(h * HEAD, (h + 1) * HEAD)
        toks = slice(t * TILE, (t + 1) * TILE)
        scores = nt(keys[low:high, cols], q[toks, cols])
        key_at = lax.broadcasted_iota(jnp.int32, scores.shape, 0) + low
        tok_at = lax.broadcasted_iota(jnp.int32, scores.shape, 1) + t * TILE
        seen = key_at > tok_at if later else key_at <= tok_at
        scores = jnp.where(seen, scores * EXP2_SCALE, -1e30)
        highest = jnp.max(scores, axis=0, keepdims=True)
        if not first:
            before = top[h, :, toks]
            highest = jnp.maximum(highest, before)
            fade = jnp.exp2(before - highest)
        weights = jnp.exp2(scores - highest)
        sums = jnp.sum(weights, axis=0, keepdims=True)
        summed = nn(values_t[cols, low:high], weights.astype(BF16))
        top[h, :, toks] = highest
        if first:
            total[h, :, toks] = sums
            acc[cols, toks] = summed
        else:
            total[h, :, toks] = fade * total[h, :, toks] + sums
            acc[cols, toks] = fade * acc[cols, toks] + summed

    for h in range(2):
        for t in range(TOK // TILE):
            token_part(k, vt, h, t, 0, (t + 1) * TILE, False, True)

    pl.semaphore_wait(ready.at[1], 2)
    tell(2)

    for copy in a_copies:
        copy.wait_recv()
    run_v = jnp.zeros((SLICE, COLS), F32)
    run_k = jnp.ones((1, COLS), F32)
    inner = []
    for b in range(GROUP):
        inner.append((run_k, run_v))
        keep = from_parts(arecv[b, SLICE:, :])
        run_v = keep * run_v + arecv[b, :SLICE, :].astype(F32)
        run_k = keep * run_k
    tsend[...] = run_v.astype(BF16)
    ktsend[...] = run_k

    def to_plane(d):
        target = (dp, jnp.minimum(zlo + d, ZLO - 1) * GROUP + r)
        return (
            remote(tsend, trecv.at[d - 1], bs_sem.at[d - 1], br_sem.at[d - 1], target),
            remote(ktsend, ktrecv.at[d - 1], bks_sem.at[d - 1], bkr_sem.at[d - 1], target),
        )

    b_copies = [to_plane(d) for d in range(1, ZLO)]
    for d in range(1, ZLO):
        if d == 5:
            pl.semaphore_wait(ready.at[2], 2)

        @pl.when(zlo + d < ZLO)
        def _():
            for copy in b_copies[d - 1]:
                copy.start()

    enter[...] = jnp.zeros_like(enter)
    gain[...] = jnp.ones_like(gain)
    for d in range(1, ZLO):

        @pl.when(zlo >= d)
        def _():
            for copy in b_copies[d - 1]:
                copy.wait_recv()
            enter[...] += gain[...] * trecv[d - 1].astype(F32)
            gain[...] = gain[...] * ktrecv[d - 1]

    for b in range(GROUP):
        inner_k, inner_v = inner[b]
        csend[b] = (inner_k * enter[...] + inner_v).astype(BF16)
    c_copies = []
    for j in range(1, GROUP):
        other, target = in_group(j)
        c_copies.append(
            remote(csend.at[other], mem.at[slice_rows], cs_sem.at[j], cr_sem.at[j], target)
        )
        c_copies[-1].start()
    mem[slice_rows, :] = csend[r]

    @pl.when(seq > 0)
    def _():
        for copy in kv_copies:
            copy.wait_recv()
        vt[...] = vprev[...].T
        for h in range(2):
            for t in range(TOK // TILE):
                token_part(kprev, vt, h, t, t * TILE, TOK, True, False)

    for copy in c_copies:
        copy.wait_recv()
    mem_t = mem[...].T
    x_rows = pl.ds(pl.multiple_of(x * COLS, COLS), COLS)
    x_copies = []
    for n in range(NCHUNK):
        toks = slice(n * CHUNK, (n + 1) * CHUNK)
        for h in range(2):
            cols = slice(h * HEAD, (h + 1) * HEAD)
            scores = nt(mem[:, cols], q[toks, cols]) * EXP2_SCALE
            before = top[h, :, toks]
            highest = jnp.maximum(jnp.max(scores, axis=0, keepdims=True), before)
            fade = jnp.exp2(before - highest)
            weights = jnp.exp2(scores - highest)
            sums = fade * total[h, :, toks] + jnp.sum(weights, axis=0, keepdims=True)
            summed = fade * acc[cols, toks] + nn(mem_t[cols, :], weights.astype(BF16))
            xatt[n, pl.ds(pl.multiple_of(x * COLS + h * HEAD, HEAD), HEAD), :] = (
                summed / sums
            ).astype(BF16)
        sent = []
        for j in (1, 3, 2):
            _, target = on_x(j)
            sent.append(
                remote(
                    xatt.at[n, x_rows], xatt.at[n, x_rows], xs_sem.at[n, j], xr_sem.at[n, j], target
                )
            )
            sent[-1].start()
        x_copies.append(sent)

    for copy in w_loads:
        copy.wait()
    for copy in w_copies:
        copy.wait_recv()
    z_copies = []
    for n in range(NCHUNK):
        for copy in x_copies[n]:
            copy.wait_recv()
        zsend[n] = nn(wbuf[1], xatt[n]).astype(BF16)
        z_copies.append(remote(zsend.at[n], zrecv.at[n], zs_sem.at[n], zr_sem.at[n], partner))
        z_copies[-1].start()
    for n in range(NCHUNK):
        own[n] = nn(wbuf[0], xatt[n])
    for n in range(NCHUNK):
        z_copies[n].wait_recv()
        o_ref[:, n * CHUNK : (n + 1) * CHUNK] = (own[n] + zrecv[n].astype(F32)).astype(BF16)

    for copy in a_copies + w_copies + c_copies + z_copies:
        copy.wait_send()
    for sent in x_copies:
        for copy in sent:
            copy.wait_send()

    @pl.when(seq < 63)
    def _():
        for copy in kv_copies:
            copy.wait_send()

    for d in range(1, ZLO):

        @pl.when(zlo + d < ZLO)
        def _():
            for copy in b_copies[d - 1]:
                copy.wait_send()


def body(queries, key_rows, value_rows, slot_queries, gate_logit, out_weight):
    dma = pltpu.SemaphoreType.DMA
    vmem = pltpu.VMEM
    return pl.pallas_call(
        kernel,
        out_shape=pltpu.VMEM((ROWS, TOK), BF16),
        in_specs=[pl.BlockSpec(memory_space=pl.ANY)] * 6,
        out_specs=pl.BlockSpec(memory_space=pltpu.VMEM),
        scratch_shapes=[
            vmem((TOK, COLS), BF16),
            vmem((TOK, COLS), BF16),
            vmem((TOK, COLS), BF16),
            vmem((STATE, COLS), BF16),
            vmem((COLS, TOK), BF16),
            vmem((TOK, COLS), BF16),
            vmem((TOK, COLS), BF16),
            vmem((1, COLS), F32),
            vmem((GROUP, SLICE + EXTRA, COLS), BF16),
            vmem((GROUP, SLICE + EXTRA, COLS), BF16),
            vmem((SLICE, COLS), BF16),
            vmem((ZLO - 1, SLICE, COLS), BF16),
            vmem((1, COLS), F32),
            vmem((ZLO - 1, 1, COLS), F32),
            vmem((SLICE, COLS), F32),
            vmem((1, COLS), F32),
            vmem((GROUP, SLICE, COLS), BF16),
            vmem((STATE, COLS), BF16),
            vmem((2, ROWS, XS * COLS), BF16),
            vmem((2, 1, TOK), F32),
            vmem((2, 1, TOK), F32),
            vmem((COLS, TOK), F32),
            vmem((NCHUNK, XS * COLS, CHUNK), BF16),
            vmem((NCHUNK, ROWS, CHUNK), BF16),
            vmem((NCHUNK, ROWS, CHUNK), BF16),
            vmem((NCHUNK, ROWS, CHUNK), F32),
            dma((5,)),
            dma((2,)),
            dma((GROUP,)),
            dma((GROUP,)),
            dma((2,)),
            dma((2,)),
            dma((XS, 2)),
            dma((XS, 2)),
            dma((ZLO - 1,)),
            dma((ZLO - 1,)),
            dma((ZLO - 1,)),
            dma((ZLO - 1,)),
            dma((GROUP,)),
            dma((GROUP,)),
            dma((NCHUNK, XS)),
            dma((NCHUNK, XS)),
            dma((NCHUNK,)),
            dma((NCHUNK,)),
            pltpu.SemaphoreType.REGULAR((3,)),
        ],
        compiler_params=pltpu.CompilerParams(collective_id=0, has_side_effects=True),
    )(queries, key_rows, value_rows, slot_queries, gate_logit, out_weight)


def solution(mesh):
    in_specs = (
        P("seq", "dp"),
        P("seq", "dp"),
        P("seq", "dp"),
        P(None, "dp"),
        P("seq", "dp"),
        P(None, "dp"),
    )
    return jax.shard_map(
        body, mesh=mesh, in_specs=in_specs, out_specs=P("dp", "seq"), check_vma=False
    )
```

```python
import functools

import jax
import jax.numpy as jnp
from jax import lax
from jax.experimental import pallas as pl
from jax.experimental.pallas import tpu as pltpu
from jax.sharding import PartitionSpec as P

HEAD = 128
MESH = pl.DeviceIdType.MESH
XS, YS, ZLO, ZS = 4, 4, 8, 16
GROUP = 8
TOK = 512
COLS = 256
STATE = 256
SLICE = STATE // GROUP
EXTRA = 16
ROWS = 256
TILE = 256
CHUNK = 128
NCHUNK = TOK // CHUNK
EXP2_SCALE = HEAD**-0.5 * 1.4426950408889634
F32 = jnp.float32
BF16 = jnp.bfloat16


def device(x, y, z, c):
    return ((z // ZLO) * XS + x, (z % ZLO) * GROUP + y * 2 + c)


def nt(a, b):
    return lax.dot_general(a, b, (((1,), (1,)), ((), ())), preferred_element_type=F32)


def nn(a, b):
    return lax.dot_general(a, b, (((1,), (0,)), ((), ())), preferred_element_type=F32)


def in_parts(rate):
    high = rate.astype(BF16)
    rest = rate - high.astype(F32)
    middle = rest.astype(BF16)
    low = (rest - middle.astype(F32)).astype(BF16)
    row = lax.broadcasted_iota(jnp.int32, (EXTRA, COLS), 0)
    wide = [jnp.broadcast_to(part.astype(F32), (EXTRA, COLS)) for part in (high, middle, low)]
    return jnp.where(row == 0, wide[0], jnp.where(row == 1, wide[1], wide[2])).astype(BF16)


def from_parts(rows):
    wide = rows.astype(F32)
    return (wide[0:1] + wide[1:2]) + wide[2:3]


def remote(src, dst, send, recv, target):
    return pltpu.make_async_remote_copy(
        src_ref=src, dst_ref=dst, send_sem=send, recv_sem=recv, device_id=target, device_id_type=MESH
    )


def kernel(
    q_hbm, k_hbm, v_hbm, sq_hbm, g_hbm, w_hbm, o_ref,
    q, k, v, sq, vt, kprev, vprev, gate, asend, arecv, tsend, trecv, ktsend, ktrecv,
    enter, gain, csend, mem, wbuf, top, total, acc, xatt, zsend, zrecv, own,
    lsem, wl_sem, as_sem, ar_sem, kvs_sem, kvr_sem, ws_sem, wr_sem,
    bs_sem, br_sem, bks_sem, bkr_sem, cs_sem, cr_sem, xs_sem, xr_sem, zs_sem, zr_sem, ready,
):
    dp = lax.axis_index("dp")
    seq = lax.axis_index("seq")
    x = dp % XS
    zlo = seq // GROUP
    z = (dp // XS) * ZLO + zlo
    r = seq % GROUP
    y = r // 2
    c = r % 2
    partner = ((dp + XS) % (2 * XS), seq)

    def in_group(j):
        other = (r + j) % GROUP
        return other, (dp, zlo * GROUP + other)

    def on_x(j):
        other = (x + j) % XS
        return other, ((dp // XS) * XS + other, seq)

    last_of_plane = (r == GROUP - 1) & (zlo < ZLO - 1)
    first_of_plane = (r == 0) & (zlo > 0)

    loads = [
        pltpu.make_async_copy(src, dst, lsem.at[i])
        for i, (src, dst) in enumerate(
            ((k_hbm, k), (sq_hbm, sq), (v_hbm, v), (g_hbm, gate), (q_hbm, q))
        )
    ]
    for copy in loads:
        copy.start()

    barrier = pltpu.get_barrier_semaphore()
    greeted = [in_group(j)[1] for j in range(1, GROUP)]
    greeted += [on_x(j)[1] for j in range(1, XS)]
    greeted += [device(x, y, (z + d) % ZS, c) for d in (1, 15)]
    for target in greeted:
        pl.semaphore_signal(barrier, inc=1, device_id=target, device_id_type=MESH)

    @pl.when(last_of_plane)
    def _():
        pl.semaphore_signal(barrier, inc=1, device_id=(dp, seq + 1), device_id_type=MESH)

    @pl.when(first_of_plane)
    def _():
        pl.semaphore_signal(barrier, inc=1, device_id=(dp, seq - 1), device_id_type=MESH)

    own_rows = pl.ds(pl.multiple_of(dp * ROWS, ROWS), ROWS)
    partner_rows = pl.ds(pl.multiple_of(partner[0] * ROWS, ROWS), ROWS)
    own_cols = pl.ds(pl.multiple_of(x * COLS, COLS), COLS)
    w_loads = [
        pltpu.make_async_copy(w_hbm.at[own_rows], wbuf.at[0, :, own_cols], wl_sem.at[0]),
        pltpu.make_async_copy(w_hbm.at[partner_rows], wbuf.at[1, :, own_cols], wl_sem.at[1]),
    ]
    for copy in w_loads:
        copy.start()

    loads[0].wait()
    loads[1].wait()
    loads[2].wait()
    loads[3].wait()
    vt[...] = v[...].T
    keep_own = jax.nn.sigmoid(gate[...])
    parts = in_parts(keep_own)
    for h in range(2):
        cols = slice(h * HEAD, (h + 1) * HEAD)
        scores = nt(k[:, cols], sq[:, cols])
        highest = jnp.max(scores, axis=0, keepdims=True)
        weights = jnp.exp2(scores * EXP2_SCALE - highest * EXP2_SCALE)
        sums = jnp.sum(weights, axis=0, keepdims=True)
        update = nn(vt[cols, :], weights.astype(BF16)) / sums
        kept = ((1.0 - keep_own[:, cols]) * update.T).astype(BF16)
        for b in range(GROUP):
            asend[b, :SLICE, cols] = kept[b * SLICE : (b + 1) * SLICE]
    for b in range(GROUP):
        asend[b, SLICE:, :] = parts

    pl.semaphore_wait(
        barrier,
        len(greeted) + last_of_plane.astype(jnp.int32) + first_of_plane.astype(jnp.int32),
    )

    def tell(n):
        for d in (1 << n, ZS - (1 << n)):
            pl.semaphore_signal(
                ready.at[n], inc=1, device_id=device(x, y, (z + d) % ZS, c), device_id_type=MESH
            )

    tell(0)
    slice_rows = pl.ds(pl.multiple_of(r * SLICE, SLICE), SLICE)
    a_copies, w_copies = [], []
    for j in (2, 6, 4, 1, 3, 5, 7):
        other, target = in_group(j)
        a_copies.append(
            remote(asend.at[other], arecv.at[r], as_sem.at[j], ar_sem.at[j], target)
        )
        a_copies[-1].start()
    for j in (1, 3, 2):
        other, target = on_x(j)
        base = (dp // XS) * XS
        for part, owner in ((0, base + other), (1, (base + XS) % (2 * XS) + other)):
            rows = pl.ds(pl.multiple_of(owner * ROWS, ROWS), ROWS)
            w_copies.append(
                remote(
                    w_hbm.at[rows], wbuf.at[part, :, own_cols],
                    ws_sem.at[j, part], wr_sem.at[j, part], target,
                )
            )
            w_copies[-1].start()

    kv_copies = [
        remote(src, dst, kvs_sem.at[i], kvr_sem.at[i], (dp, jnp.minimum(seq + 1, 63)))
        for i, (src, dst) in enumerate(((k_hbm, kprev), (v_hbm, vprev)))
    ]

    @pl.when(seq < 63)
    def _():
        for copy in kv_copies:
            copy.start()

    arecv[r] = asend[r]

    pl.semaphore_wait(ready.at[0], 2)
    tell(1)

    loads[4].wait()

    def token_part(keys, values_t, h, t, low, high, later, first):
        cols = slice(h * HEAD, (h + 1) * HEAD)
        toks = slice(t * TILE, (t + 1) * TILE)
        scores = nt(keys[low:high, cols], q[toks, cols])
        key_at = lax.broadcasted_iota(jnp.int32, scores.shape, 0) + low
        tok_at = lax.broadcasted_iota(jnp.int32, scores.shape, 1) + t * TILE
        seen = key_at > tok_at if later else key_at <= tok_at
        scores = jnp.where(seen, scores * EXP2_SCALE, -1e30)
        highest = jnp.max(scores, axis=0, keepdims=True)
        if not first:
            before = top[h, :, toks]
            highest = jnp.maximum(highest, before)
            fade = jnp.exp2(before - highest)
        weights = jnp.exp2(scores - highest)
        sums = jnp.sum(weights, axis=0, keepdims=True)
        summed = nn(values_t[cols, low:high], weights.astype(BF16))
        top[h, :, toks] = highest
        if first:
            total[h, :, toks] = sums
            acc[cols, toks] = summed
        else:
            total[h, :, toks] = fade * total[h, :, toks] + sums
            acc[cols, toks] = fade * acc[cols, toks] + summed

    for h in range(2):
        for t in range(TOK // TILE):
            token_part(k, vt, h, t, 0, (t + 1) * TILE, False, True)

    pl.semaphore_wait(ready.at[1], 2)
    tell(2)

    for copy in a_copies:
        copy.wait_recv()
    run_v = jnp.zeros((SLICE, COLS), F32)
    run_k = jnp.ones((1, COLS), F32)
    inner = []
    for b in range(GROUP):
        inner.append((run_k, run_v))
        keep = from_parts(arecv[b, SLICE:, :])
        run_v = keep * run_v + arecv[b, :SLICE, :].astype(F32)
        run_k = keep * run_k
    tsend[...] = run_v.astype(BF16)
    ktsend[...] = run_k

    def to_plane(d):
        target = (dp, jnp.minimum(zlo + d, ZLO - 1) * GROUP + r)
        return (
            remote(tsend, trecv.at[d - 1], bs_sem.at[d - 1], br_sem.at[d - 1], target),
            remote(ktsend, ktrecv.at[d - 1], bks_sem.at[d - 1], bkr_sem.at[d - 1], target),
        )

    b_copies = [to_plane(d) for d in range(1, ZLO)]
    for d in range(1, ZLO):
        if d == 5:
            pl.semaphore_wait(ready.at[2], 2)

        @pl.when(zlo + d < ZLO)
        def _():
            for copy in b_copies[d - 1]:
                copy.start()

    enter[...] = jnp.zeros_like(enter)
    gain[...] = jnp.ones_like(gain)
    for d in range(1, ZLO):

        @pl.when(zlo >= d)
        def _():
            for copy in b_copies[d - 1]:
                copy.wait_recv()
            enter[...] += gain[...] * trecv[d - 1].astype(F32)
            gain[...] = gain[...] * ktrecv[d - 1]

    for b in range(GROUP):
        inner_k, inner_v = inner[b]
        csend[b] = (inner_k * enter[...] + inner_v).astype(BF16)
    c_copies = []
    for j in (2, 6, 4, 1, 7, 3, 5):
        other, target = in_group(j)
        c_copies.append(
            remote(csend.at[other], mem.at[slice_rows], cs_sem.at[j], cr_sem.at[j], target)
        )
        c_copies[-1].start()
    mem[slice_rows, :] = csend[r]

    @pl.when(seq > 0)
    def _():
        for copy in kv_copies:
            copy.wait_recv()
        vt[...] = vprev[...].T
        for h in range(2):
            for t in range(TOK // TILE):
                token_part(kprev, vt, h, t, t * TILE, TOK, True, False)

    for copy in c_copies:
        copy.wait_recv()
    mem_t = mem[...].T
    x_rows = pl.ds(pl.multiple_of(x * COLS, COLS), COLS)
    x_copies = []
    for n in range(NCHUNK):
        toks = slice(n * CHUNK, (n + 1) * CHUNK)
        for h in range(2):
            cols = slice(h * HEAD, (h + 1) * HEAD)
            scores = nt(mem[:, cols], q[toks, cols]) * EXP2_SCALE
            before = top[h, :, toks]
            highest = jnp.maximum(jnp.max(scores, axis=0, keepdims=True), before)
            fade = jnp.exp2(before - highest)
            weights = jnp.exp2(scores - highest)
            sums = fade * total[h, :, toks] + jnp.sum(weights, axis=0, keepdims=True)
            summed = fade * acc[cols, toks] + nn(mem_t[cols, :], weights.astype(BF16))
            xatt[n, pl.ds(pl.multiple_of(x * COLS + h * HEAD, HEAD), HEAD), :] = (
                summed / sums
            ).astype(BF16)
        sent = []
        for j in (1, 3, 2):
            _, target = on_x(j)
            sent.append(
                remote(
                    xatt.at[n, x_rows], xatt.at[n, x_rows], xs_sem.at[n, j], xr_sem.at[n, j], target
                )
            )
            sent[-1].start()
        x_copies.append(sent)

    for copy in w_loads:
        copy.wait()
    for copy in w_copies:
        copy.wait_recv()
    z_copies = []
    for n in range(NCHUNK):
        for copy in x_copies[n]:
            copy.wait_recv()
        zsend[n] = nn(wbuf[1], xatt[n]).astype(BF16)
        z_copies.append(remote(zsend.at[n], zrecv.at[n], zs_sem.at[n], zr_sem.at[n], partner))
        z_copies[-1].start()
    for n in range(NCHUNK):
        own[n] = nn(wbuf[0], xatt[n])
    for n in range(NCHUNK):
        z_copies[n].wait_recv()
        o_ref[:, n * CHUNK : (n + 1) * CHUNK] = (own[n] + zrecv[n].astype(F32)).astype(BF16)

    for copy in a_copies + w_copies + c_copies + z_copies:
        copy.wait_send()
    for sent in x_copies:
        for copy in sent:
            copy.wait_send()

    @pl.when(seq < 63)
    def _():
        for copy in kv_copies:
            copy.wait_send()

    for d in range(1, ZLO):

        @pl.when(zlo + d < ZLO)
        def _():
            for copy in b_copies[d - 1]:
                copy.wait_send()


def body(queries, key_rows, value_rows, slot_queries, gate_logit, out_weight):
    dma = pltpu.SemaphoreType.DMA
    vmem = pltpu.VMEM
    return pl.pallas_call(
        kernel,
        out_shape=pltpu.VMEM((ROWS, TOK), BF16),
        in_specs=[pl.BlockSpec(memory_space=pl.ANY)] * 6,
        out_specs=pl.BlockSpec(memory_space=pltpu.VMEM),
        scratch_shapes=[
            vmem((TOK, COLS), BF16),
            vmem((TOK, COLS), BF16),
            vmem((TOK, COLS), BF16),
            vmem((STATE, COLS), BF16),
            vmem((COLS, TOK), BF16),
            vmem((TOK, COLS), BF16),
            vmem((TOK, COLS), BF16),
            vmem((1, COLS), F32),
            vmem((GROUP, SLICE + EXTRA, COLS), BF16),
            vmem((GROUP, SLICE + EXTRA, COLS), BF16),
            vmem((SLICE, COLS), BF16),
            vmem((ZLO - 1, SLICE, COLS), BF16),
            vmem((1, COLS), F32),
            vmem((ZLO - 1, 1, COLS), F32),
            vmem((SLICE, COLS), F32),
            vmem((1, COLS), F32),
            vmem((GROUP, SLICE, COLS), BF16),
            vmem((STATE, COLS), BF16),
            vmem((2, ROWS, XS * COLS), BF16),
            vmem((2, 1, TOK), F32),
            vmem((2, 1, TOK), F32),
            vmem((COLS, TOK), F32),
            vmem((NCHUNK, XS * COLS, CHUNK), BF16),
            vmem((NCHUNK, ROWS, CHUNK), BF16),
            vmem((NCHUNK, ROWS, CHUNK), BF16),
            vmem((NCHUNK, ROWS, CHUNK), F32),
            dma((5,)),
            dma((2,)),
            dma((GROUP,)),
            dma((GROUP,)),
            dma((2,)),
            dma((2,)),
            dma((XS, 2)),
            dma((XS, 2)),
            dma((ZLO - 1,)),
            dma((ZLO - 1,)),
            dma((ZLO - 1,)),
            dma((ZLO - 1,)),
            dma((GROUP,)),
            dma((GROUP,)),
            dma((NCHUNK, XS)),
            dma((NCHUNK, XS)),
            dma((NCHUNK,)),
            dma((NCHUNK,)),
            pltpu.SemaphoreType.REGULAR((3,)),
        ],
        compiler_params=pltpu.CompilerParams(collective_id=0, has_side_effects=True),
    )(queries, key_rows, value_rows, slot_queries, gate_logit, out_weight)


def solution(mesh):
    in_specs = (
        P("seq", "dp"),
        P("seq", "dp"),
        P("seq", "dp"),
        P(None, "dp"),
        P("seq", "dp"),
        P(None, "dp"),
    )
    return jax.shard_map(
        body, mesh=mesh, in_specs=in_specs, out_specs=P("dp", "seq"), check_vma=False
    )
```

```python
import functools

import jax
import jax.numpy as jnp
from jax import lax
from jax.experimental import pallas as pl
from jax.experimental.pallas import tpu as pltpu
from jax.sharding import PartitionSpec as P

HEAD = 128
MESH = pl.DeviceIdType.MESH
XS, YS, ZLO, ZS = 4, 4, 8, 16
GROUP = 8
QUAD = 4
TOK = 512
COLS = 256
STATE = 256
SLICE = STATE // GROUP
EXTRA = 16
ROWS = 256
TILE = 256
CHUNK = 128
NCHUNK = TOK // CHUNK
EXP2_SCALE = HEAD**-0.5 * 1.4426950408889634
F32 = jnp.float32
BF16 = jnp.bfloat16


def device(x, y, z, c):
    return ((z // ZLO) * XS + x, (z % ZLO) * GROUP + y * 2 + c)


def nt(a, b):
    return lax.dot_general(a, b, (((1,), (1,)), ((), ())), preferred_element_type=F32)


def nn(a, b):
    return lax.dot_general(a, b, (((1,), (0,)), ((), ())), preferred_element_type=F32)


def in_parts(rate):
    high = rate.astype(BF16)
    rest = rate - high.astype(F32)
    middle = rest.astype(BF16)
    low = (rest - middle.astype(F32)).astype(BF16)
    row = lax.broadcasted_iota(jnp.int32, (EXTRA, COLS), 0)
    wide = [jnp.broadcast_to(part.astype(F32), (EXTRA, COLS)) for part in (high, middle, low)]
    return jnp.where(row == 0, wide[0], jnp.where(row == 1, wide[1], wide[2])).astype(BF16)


def from_parts(rows):
    wide = rows.astype(F32)
    return (wide[0:1] + wide[1:2]) + wide[2:3]


def remote(src, dst, send, recv, target):
    return pltpu.make_async_remote_copy(
        src_ref=src, dst_ref=dst, send_sem=send, recv_sem=recv, device_id=target, device_id_type=MESH
    )


def kernel(
    q_hbm, k_hbm, v_hbm, sq_hbm, g_hbm, w_hbm, o_ref,
    q, k, v, sq, vt, kprev, vprev, gate, asend, arecv, tsend, trecv, ktsend, ktrecv, usend, urecv,
    enter, gain, csend, mem, wbuf, top, total, acc, xatt, zsend, zrecv, own,
    lsem, wl_sem, as_sem, ar_sem, kvs_sem, kvr_sem, ws_sem, wr_sem,
    bs_sem, br_sem, bks_sem, bkr_sem, us_sem, ur_sem, cs_sem, cr_sem, xs_sem, xr_sem, zs_sem, zr_sem, ready,
):
    dp = lax.axis_index("dp")
    seq = lax.axis_index("seq")
    x = dp % XS
    zlo = seq // GROUP
    z = (dp // XS) * ZLO + zlo
    r = seq % GROUP
    y = r // 2
    c = r % 2
    partner = ((dp + XS) % (2 * XS), seq)

    def in_group(j):
        other = (r + j) % GROUP
        return other, (dp, zlo * GROUP + other)

    def on_x(j):
        other = (x + j) % XS
        return other, ((dp // XS) * XS + other, seq)

    last_of_plane = (r == GROUP - 1) & (zlo < ZLO - 1)
    first_of_plane = (r == 0) & (zlo > 0)

    loads = [
        pltpu.make_async_copy(src, dst, lsem.at[i])
        for i, (src, dst) in enumerate(
            ((k_hbm, k), (sq_hbm, sq), (v_hbm, v), (g_hbm, gate), (q_hbm, q))
        )
    ]
    for copy in loads:
        copy.start()

    barrier = pltpu.get_barrier_semaphore()
    greeted = [in_group(j)[1] for j in range(1, GROUP)]
    greeted += [on_x(j)[1] for j in range(1, XS)]
    greeted += [device(x, y, (z + d) % ZS, c) for d in (1, 15)]
    for target in greeted:
        pl.semaphore_signal(barrier, inc=1, device_id=target, device_id_type=MESH)

    @pl.when(last_of_plane)
    def _():
        pl.semaphore_signal(barrier, inc=1, device_id=(dp, seq + 1), device_id_type=MESH)

    @pl.when(first_of_plane)
    def _():
        pl.semaphore_signal(barrier, inc=1, device_id=(dp, seq - 1), device_id_type=MESH)

    own_rows = pl.ds(pl.multiple_of(dp * ROWS, ROWS), ROWS)
    partner_rows = pl.ds(pl.multiple_of(partner[0] * ROWS, ROWS), ROWS)
    own_cols = pl.ds(pl.multiple_of(x * COLS, COLS), COLS)
    w_loads = [
        pltpu.make_async_copy(w_hbm.at[own_rows], wbuf.at[0, :, own_cols], wl_sem.at[0]),
        pltpu.make_async_copy(w_hbm.at[partner_rows], wbuf.at[1, :, own_cols], wl_sem.at[1]),
    ]
    for copy in w_loads:
        copy.start()

    loads[0].wait()
    loads[1].wait()
    loads[2].wait()
    loads[3].wait()
    vt[...] = v[...].T
    keep_own = jax.nn.sigmoid(gate[...])
    parts = in_parts(keep_own)
    for h in range(2):
        cols = slice(h * HEAD, (h + 1) * HEAD)
        scores = nt(k[:, cols], sq[:, cols])
        highest = jnp.max(scores, axis=0, keepdims=True)
        weights = jnp.exp2(scores * EXP2_SCALE - highest * EXP2_SCALE)
        sums = jnp.sum(weights, axis=0, keepdims=True)
        update = nn(vt[cols, :], weights.astype(BF16)) / sums
        kept = ((1.0 - keep_own[:, cols]) * update.T).astype(BF16)
        for b in range(GROUP):
            asend[b, :SLICE, cols] = kept[b * SLICE : (b + 1) * SLICE]
    for b in range(GROUP):
        asend[b, SLICE:, :] = parts

    pl.semaphore_wait(
        barrier,
        len(greeted) + last_of_plane.astype(jnp.int32) + first_of_plane.astype(jnp.int32),
    )

    def tell(n):
        for d in (1 << n, ZS - (1 << n)):
            pl.semaphore_signal(
                ready.at[n], inc=1, device_id=device(x, y, (z + d) % ZS, c), device_id_type=MESH
            )

    tell(0)
    slice_rows = pl.ds(pl.multiple_of(r * SLICE, SLICE), SLICE)
    a_copies, w_copies = [], []
    for j in (2, 6, 4, 1, 3, 5, 7):
        other, target = in_group(j)
        a_copies.append(
            remote(asend.at[other], arecv.at[r], as_sem.at[j], ar_sem.at[j], target)
        )
        a_copies[-1].start()
    for j in (1, 3, 2):
        other, target = on_x(j)
        base = (dp // XS) * XS
        for part, owner in ((0, base + other), (1, (base + XS) % (2 * XS) + other)):
            rows = pl.ds(pl.multiple_of(owner * ROWS, ROWS), ROWS)
            w_copies.append(
                remote(
                    w_hbm.at[rows], wbuf.at[part, :, own_cols],
                    ws_sem.at[j, part], wr_sem.at[j, part], target,
                )
            )
            w_copies[-1].start()

    kv_copies = [
        remote(src, dst, kvs_sem.at[i], kvr_sem.at[i], (dp, jnp.minimum(seq + 1, 63)))
        for i, (src, dst) in enumerate(((k_hbm, kprev), (v_hbm, vprev)))
    ]

    @pl.when(seq < 63)
    def _():
        for copy in kv_copies:
            copy.start()

    arecv[r] = asend[r]

    pl.semaphore_wait(ready.at[0], 2)
    tell(1)

    loads[4].wait()

    def token_part(keys, values_t, h, t, low, high, later, first):
        cols = slice(h * HEAD, (h + 1) * HEAD)
        toks = slice(t * TILE, (t + 1) * TILE)
        scores = nt(keys[low:high, cols], q[toks, cols])
        key_at = lax.broadcasted_iota(jnp.int32, scores.shape, 0) + low
        tok_at = lax.broadcasted_iota(jnp.int32, scores.shape, 1) + t * TILE
        seen = key_at > tok_at if later else key_at <= tok_at
        scores = jnp.where(seen, scores * EXP2_SCALE, -1e30)
        highest = jnp.max(scores, axis=0, keepdims=True)
        if not first:
            before = top[h, :, toks]
            highest = jnp.maximum(highest, before)
            fade = jnp.exp2(before - highest)
        weights = jnp.exp2(scores - highest)
        sums = jnp.sum(weights, axis=0, keepdims=True)
        summed = nn(values_t[cols, low:high], weights.astype(BF16))
        top[h, :, toks] = highest
        if first:
            total[h, :, toks] = sums
            acc[cols, toks] = summed
        else:
            total[h, :, toks] = fade * total[h, :, toks] + sums
            acc[cols, toks] = fade * acc[cols, toks] + summed

    for h in range(2):
        for t in range(TOK // TILE):
            token_part(k, vt, h, t, 0, (t + 1) * TILE, False, True)

    pl.semaphore_wait(ready.at[1], 2)
    tell(2)

    for copy in a_copies:
        copy.wait_recv()
    run_v = jnp.zeros((SLICE, COLS), F32)
    run_k = jnp.ones((1, COLS), F32)
    inner = []
    for b in range(GROUP):
        inner.append((run_k, run_v))
        keep = from_parts(arecv[b, SLICE:, :])
        run_v = keep * run_v + arecv[b, :SLICE, :].astype(F32)
        run_k = keep * run_k
    tsend[...] = run_v.astype(BF16)
    ktsend[...] = run_k

    def to_plane(d):
        target = (dp, jnp.minimum(zlo + d, ZLO - 1) * GROUP + r)
        return (
            remote(tsend, trecv.at[d - 1], bs_sem.at[d - 1], br_sem.at[d - 1], target),
            remote(ktsend, ktrecv.at[d - 1], bks_sem.at[d - 1], bkr_sem.at[d - 1], target),
        )

    b_copies = [to_plane(d) for d in range(1, QUAD)]
    u_copies = [
        remote(
            usend, urecv, us_sem.at[d - 1], ur_sem.at[d - 1],
            (dp, jnp.minimum(zlo + d, ZLO - 1) * GROUP + r),
        )
        for d in range(1, QUAD + 1)
    ]
    place = zlo % QUAD
    for d in range(1, QUAD):

        @pl.when(place + d < QUAD)
        def _():
            for copy in b_copies[d - 1]:
                copy.start()

    enter[...] = jnp.zeros_like(enter)
    gain[...] = jnp.ones_like(gain)
    for d in range(1, QUAD):

        @pl.when(place >= d)
        def _():
            for copy in b_copies[d - 1]:
                copy.wait_recv()
            enter[...] += gain[...] * trecv[d - 1].astype(F32)
            gain[...] = gain[...] * ktrecv[d - 1]

    @pl.when(zlo == QUAD - 1)
    def _():
        usend[...] = (run_k * enter[...] + run_v).astype(BF16)
        for copy in u_copies:
            copy.start()

    for d in range(1, QUAD + 1):

        @pl.when(zlo == QUAD - 1 + d)
        def _():
            u_copies[d - 1].wait_recv()
            enter[...] += gain[...] * urecv[...].astype(F32)

    for b in range(GROUP):
        inner_k, inner_v = inner[b]
        csend[b] = (inner_k * enter[...] + inner_v).astype(BF16)
    c_copies = []
    for j in (2, 6, 4, 1, 7, 3, 5):
        other, target = in_group(j)
        c_copies.append(
            remote(csend.at[other], mem.at[slice_rows], cs_sem.at[j], cr_sem.at[j], target)
        )
        c_copies[-1].start()
    mem[slice_rows, :] = csend[r]
    pl.semaphore_wait(ready.at[2], 2)

    @pl.when(seq > 0)
    def _():
        for copy in kv_copies:
            copy.wait_recv()
        vt[...] = vprev[...].T
        for h in range(2):
            for t in range(TOK // TILE):
                token_part(kprev, vt, h, t, t * TILE, TOK, True, False)

    for copy in c_copies:
        copy.wait_recv()
    mem_t = mem[...].T
    x_rows = pl.ds(pl.multiple_of(x * COLS, COLS), COLS)
    x_copies = []
    for n in range(NCHUNK):
        toks = slice(n * CHUNK, (n + 1) * CHUNK)
        for h in range(2):
            cols = slice(h * HEAD, (h + 1) * HEAD)
            scores = nt(mem[:, cols], q[toks, cols]) * EXP2_SCALE
            before = top[h, :, toks]
            highest = jnp.maximum(jnp.max(scores, axis=0, keepdims=True), before)
            fade = jnp.exp2(before - highest)
            weights = jnp.exp2(scores - highest)
            sums = fade * total[h, :, toks] + jnp.sum(weights, axis=0, keepdims=True)
            summed = fade * acc[cols, toks] + nn(mem_t[cols, :], weights.astype(BF16))
            xatt[n, pl.ds(pl.multiple_of(x * COLS + h * HEAD, HEAD), HEAD), :] = (
                summed / sums
            ).astype(BF16)
        sent = []
        for j in (1, 3, 2):
            _, target = on_x(j)
            sent.append(
                remote(
                    xatt.at[n, x_rows], xatt.at[n, x_rows], xs_sem.at[n, j], xr_sem.at[n, j], target
                )
            )
            sent[-1].start()
        x_copies.append(sent)

    for copy in w_loads:
        copy.wait()
    for copy in w_copies:
        copy.wait_recv()
    z_copies = []
    for n in range(NCHUNK):
        for copy in x_copies[n]:
            copy.wait_recv()
        zsend[n] = nn(wbuf[1], xatt[n]).astype(BF16)
        z_copies.append(remote(zsend.at[n], zrecv.at[n], zs_sem.at[n], zr_sem.at[n], partner))
        z_copies[-1].start()
    for n in range(NCHUNK):
        own[n] = nn(wbuf[0], xatt[n])
    for n in range(NCHUNK):
        z_copies[n].wait_recv()
        o_ref[:, n * CHUNK : (n + 1) * CHUNK] = (own[n] + zrecv[n].astype(F32)).astype(BF16)

    for copy in a_copies + w_copies + c_copies + z_copies:
        copy.wait_send()
    for sent in x_copies:
        for copy in sent:
            copy.wait_send()

    @pl.when(seq < 63)
    def _():
        for copy in kv_copies:
            copy.wait_send()

    for d in range(1, QUAD):

        @pl.when(place + d < QUAD)
        def _():
            for copy in b_copies[d - 1]:
                copy.wait_send()

    @pl.when(zlo == QUAD - 1)
    def _():
        for copy in u_copies:
            copy.wait_send()


def body(queries, key_rows, value_rows, slot_queries, gate_logit, out_weight):
    dma = pltpu.SemaphoreType.DMA
    vmem = pltpu.VMEM
    return pl.pallas_call(
        kernel,
        out_shape=pltpu.VMEM((ROWS, TOK), BF16),
        in_specs=[pl.BlockSpec(memory_space=pl.ANY)] * 6,
        out_specs=pl.BlockSpec(memory_space=pltpu.VMEM),
        scratch_shapes=[
            vmem((TOK, COLS), BF16),
            vmem((TOK, COLS), BF16),
            vmem((TOK, COLS), BF16),
            vmem((STATE, COLS), BF16),
            vmem((COLS, TOK), BF16),
            vmem((TOK, COLS), BF16),
            vmem((TOK, COLS), BF16),
            vmem((1, COLS), F32),
            vmem((GROUP, SLICE + EXTRA, COLS), BF16),
            vmem((GROUP, SLICE + EXTRA, COLS), BF16),
            vmem((SLICE, COLS), BF16),
            vmem((QUAD - 1, SLICE, COLS), BF16),
            vmem((1, COLS), F32),
            vmem((QUAD - 1, 1, COLS), F32),
            vmem((SLICE, COLS), BF16),
            vmem((SLICE, COLS), BF16),
            vmem((SLICE, COLS), F32),
            vmem((1, COLS), F32),
            vmem((GROUP, SLICE, COLS), BF16),
            vmem((STATE, COLS), BF16),
            vmem((2, ROWS, XS * COLS), BF16),
            vmem((2, 1, TOK), F32),
            vmem((2, 1, TOK), F32),
            vmem((COLS, TOK), F32),
            vmem((NCHUNK, XS * COLS, CHUNK), BF16),
            vmem((NCHUNK, ROWS, CHUNK), BF16),
            vmem((NCHUNK, ROWS, CHUNK), BF16),
            vmem((NCHUNK, ROWS, CHUNK), F32),
            dma((5,)),
            dma((2,)),
            dma((GROUP,)),
            dma((GROUP,)),
            dma((2,)),
            dma((2,)),
            dma((XS, 2)),
            dma((XS, 2)),
            dma((QUAD - 1,)),
            dma((QUAD - 1,)),
            dma((QUAD - 1,)),
            dma((QUAD - 1,)),
            dma((QUAD,)),
            dma((QUAD,)),
            dma((GROUP,)),
            dma((GROUP,)),
            dma((NCHUNK, XS)),
            dma((NCHUNK, XS)),
            dma((NCHUNK,)),
            dma((NCHUNK,)),
            pltpu.SemaphoreType.REGULAR((3,)),
        ],
        compiler_params=pltpu.CompilerParams(collective_id=0, has_side_effects=True),
    )(queries, key_rows, value_rows, slot_queries, gate_logit, out_weight)


def solution(mesh):
    in_specs = (
        P("seq", "dp"),
        P("seq", "dp"),
        P("seq", "dp"),
        P(None, "dp"),
        P("seq", "dp"),
        P(None, "dp"),
    )
    return jax.shard_map(
        body, mesh=mesh, in_specs=in_specs, out_specs=P("dp", "seq"), check_vma=False
    )
```

```python
import functools

import jax
import jax.numpy as jnp
from jax import lax
from jax.experimental import pallas as pl
from jax.experimental.pallas import tpu as pltpu
from jax.sharding import PartitionSpec as P

HEAD = 128
MESH = pl.DeviceIdType.MESH
XS, YS, ZLO, ZS = 4, 4, 8, 16
GROUP = 8
QUAD = 4
TOK = 512
COLS = 256
STATE = 256
SLICE = STATE // GROUP
EXTRA = 16
ROWS = 256
TILE = 256
CHUNK = 128
NCHUNK = TOK // CHUNK
EXP2_SCALE = HEAD**-0.5 * 1.4426950408889634
F32 = jnp.float32
BF16 = jnp.bfloat16


def device(x, y, z, c):
    return ((z // ZLO) * XS + x, (z % ZLO) * GROUP + y * 2 + c)


def nt(a, b):
    return lax.dot_general(a, b, (((1,), (1,)), ((), ())), preferred_element_type=F32)


def nn(a, b):
    return lax.dot_general(a, b, (((1,), (0,)), ((), ())), preferred_element_type=F32)


def in_parts(rate):
    high = rate.astype(BF16)
    rest = rate - high.astype(F32)
    middle = rest.astype(BF16)
    low = (rest - middle.astype(F32)).astype(BF16)
    row = lax.broadcasted_iota(jnp.int32, (EXTRA, COLS), 0)
    wide = [jnp.broadcast_to(part.astype(F32), (EXTRA, COLS)) for part in (high, middle, low)]
    return jnp.where(row == 0, wide[0], jnp.where(row == 1, wide[1], wide[2])).astype(BF16)


def from_parts(rows):
    wide = rows.astype(F32)
    return (wide[0:1] + wide[1:2]) + wide[2:3]


def remote(src, dst, send, recv, target):
    return pltpu.make_async_remote_copy(
        src_ref=src, dst_ref=dst, send_sem=send, recv_sem=recv, device_id=target, device_id_type=MESH
    )


def kernel(
    q_hbm, k_hbm, v_hbm, sq_hbm, g_hbm, w_hbm, o_ref,
    q, k, v, sq, vt, kprev, vprev, gate, asend, arecv, tsend, trecv, ktsend, ktrecv, usend, urecv,
    enter, gain, csend, mem, wbuf, top, total, acc, xatt, zsend, zrecv, own,
    lsem, wl_sem, as_sem, ar_sem, kvs_sem, kvr_sem, ws_sem, wr_sem,
    bs_sem, br_sem, bks_sem, bkr_sem, us_sem, ur_sem, cs_sem, cr_sem, xs_sem, xr_sem, zs_sem, zr_sem, ready,
):
    dp = lax.axis_index("dp")
    seq = lax.axis_index("seq")
    x = dp % XS
    zlo = seq // GROUP
    z = (dp // XS) * ZLO + zlo
    r = seq % GROUP
    y = r // 2
    c = r % 2
    partner = ((dp + XS) % (2 * XS), seq)

    def in_group(j):
        other = (r + j) % GROUP
        return other, (dp, zlo * GROUP + other)

    def on_x(j):
        other = (x + j) % XS
        return other, ((dp // XS) * XS + other, seq)

    last_of_plane = (r == GROUP - 1) & (zlo < ZLO - 1)
    first_of_plane = (r == 0) & (zlo > 0)

    loads = [
        pltpu.make_async_copy(src, dst, lsem.at[i])
        for i, (src, dst) in enumerate(
            ((k_hbm, k), (sq_hbm, sq), (v_hbm, v), (g_hbm, gate), (q_hbm, q))
        )
    ]
    for copy in loads:
        copy.start()

    barrier = pltpu.get_barrier_semaphore()
    greeted = [in_group(j)[1] for j in range(1, GROUP)]
    greeted += [on_x(j)[1] for j in range(1, XS)]
    greeted += [device(x, y, (z + d) % ZS, c) for d in (1, 15)]
    for target in greeted:
        pl.semaphore_signal(barrier, inc=1, device_id=target, device_id_type=MESH)

    @pl.when(last_of_plane)
    def _():
        pl.semaphore_signal(barrier, inc=1, device_id=(dp, seq + 1), device_id_type=MESH)

    @pl.when(first_of_plane)
    def _():
        pl.semaphore_signal(barrier, inc=1, device_id=(dp, seq - 1), device_id_type=MESH)

    own_rows = pl.ds(pl.multiple_of(dp * ROWS, ROWS), ROWS)
    partner_rows = pl.ds(pl.multiple_of(partner[0] * ROWS, ROWS), ROWS)
    own_cols = pl.ds(pl.multiple_of(x * COLS, COLS), COLS)
    w_loads = [
        pltpu.make_async_copy(w_hbm.at[own_rows], wbuf.at[0, :, own_cols], wl_sem.at[0]),
        pltpu.make_async_copy(w_hbm.at[partner_rows], wbuf.at[1, :, own_cols], wl_sem.at[1]),
    ]
    for copy in w_loads:
        copy.start()

    loads[0].wait()
    loads[1].wait()
    loads[2].wait()
    loads[3].wait()
    vt[...] = v[...].T
    keep_own = jax.nn.sigmoid(gate[...])
    parts = in_parts(keep_own)
    for h in range(2):
        cols = slice(h * HEAD, (h + 1) * HEAD)
        scores = nt(k[:, cols], sq[:, cols])
        highest = jnp.max(scores, axis=0, keepdims=True)
        weights = jnp.exp2(scores * EXP2_SCALE - highest * EXP2_SCALE)
        sums = jnp.sum(weights, axis=0, keepdims=True)
        update = nn(vt[cols, :], weights.astype(BF16)) / sums
        kept = ((1.0 - keep_own[:, cols]) * update.T).astype(BF16)
        for b in range(GROUP):
            asend[b, :SLICE, cols] = kept[b * SLICE : (b + 1) * SLICE]
    for b in range(GROUP):
        asend[b, SLICE:, :] = parts

    pl.semaphore_wait(
        barrier,
        len(greeted) + last_of_plane.astype(jnp.int32) + first_of_plane.astype(jnp.int32),
    )

    def tell(n):
        for d in (1 << n, ZS - (1 << n)):
            pl.semaphore_signal(
                ready.at[n], inc=1, device_id=device(x, y, (z + d) % ZS, c), device_id_type=MESH
            )

    tell(0)
    slice_rows = pl.ds(pl.multiple_of(r * SLICE, SLICE), SLICE)
    a_copies, w_copies = [], []
    for j in (2, 6, 4, 1, 3, 5, 7):
        other, target = in_group(j)
        a_copies.append(
            remote(asend.at[other], arecv.at[r], as_sem.at[j], ar_sem.at[j], target)
        )
        a_copies[-1].start()
    for j in (1, 3, 2):
        other, target = on_x(j)
        base = (dp // XS) * XS
        for part, owner in ((0, base + other), (1, (base + XS) % (2 * XS) + other)):
            rows = pl.ds(pl.multiple_of(owner * ROWS, ROWS), ROWS)
            w_copies.append(
                remote(
                    w_hbm.at[rows], wbuf.at[part, :, own_cols],
                    ws_sem.at[j, part], wr_sem.at[j, part], target,
                )
            )
            w_copies[-1].start()

    kv_copies = [
        remote(src, dst, kvs_sem.at[i], kvr_sem.at[i], (dp, jnp.minimum(seq + 1, 63)))
        for i, (src, dst) in enumerate(((k_hbm, kprev), (v_hbm, vprev)))
    ]

    @pl.when(seq < 63)
    def _():
        for copy in kv_copies:
            copy.start()

    arecv[r] = asend[r]

    pl.semaphore_wait(ready.at[0], 2)
    tell(1)

    loads[4].wait()

    def token_part(keys, values_t, h, t, low, high, later, first):
        cols = slice(h * HEAD, (h + 1) * HEAD)
        toks = slice(t * TILE, (t + 1) * TILE)
        scores = nt(keys[low:high, cols], q[toks, cols])
        key_at = lax.broadcasted_iota(jnp.int32, scores.shape, 0) + low
        tok_at = lax.broadcasted_iota(jnp.int32, scores.shape, 1) + t * TILE
        seen = key_at > tok_at if later else key_at <= tok_at
        scores = jnp.where(seen, scores * EXP2_SCALE, -1e30)
        highest = jnp.max(scores, axis=0, keepdims=True)
        if not first:
            before = top[h, :, toks]
            highest = jnp.maximum(highest, before)
            fade = jnp.exp2(before - highest)
        weights = jnp.exp2(scores - highest)
        sums = jnp.sum(weights, axis=0, keepdims=True)
        summed = nn(values_t[cols, low:high], weights.astype(BF16))
        top[h, :, toks] = highest
        if first:
            total[h, :, toks] = sums
            acc[cols, toks] = summed
        else:
            total[h, :, toks] = fade * total[h, :, toks] + sums
            acc[cols, toks] = fade * acc[cols, toks] + summed

    for h in range(2):
        for t in range(TOK // TILE):
            token_part(k, vt, h, t, 0, (t + 1) * TILE, False, True)

    pl.semaphore_wait(ready.at[1], 2)
    tell(2)

    for copy in a_copies:
        copy.wait_recv()
    run_v = jnp.zeros((SLICE, COLS), F32)
    run_k = jnp.ones((1, COLS), F32)
    inner = []
    for b in range(GROUP):
        inner.append((run_k, run_v))
        keep = from_parts(arecv[b, SLICE:, :])
        run_v = keep * run_v + arecv[b, :SLICE, :].astype(F32)
        run_k = keep * run_k
    tsend[...] = run_v.astype(BF16)
    ktsend[...] = run_k

    def to_plane(d):
        target = (dp, jnp.minimum(zlo + d, ZLO - 1) * GROUP + r)
        return (
            remote(tsend, trecv.at[d - 1], bs_sem.at[d - 1], br_sem.at[d - 1], target),
            remote(ktsend, ktrecv.at[d - 1], bks_sem.at[d - 1], bkr_sem.at[d - 1], target),
        )

    b_copies = [to_plane(d) for d in range(1, QUAD)]
    u_copies = [
        remote(
            usend, urecv, us_sem.at[d - 1], ur_sem.at[d - 1],
            (dp, jnp.minimum(zlo + d, ZLO - 1) * GROUP + r),
        )
        for d in range(1, QUAD + 1)
    ]
    place = zlo % QUAD
    for d in range(1, QUAD):

        @pl.when(place + d < QUAD)
        def _():
            for copy in b_copies[d - 1]:
                copy.start()

    enter[...] = jnp.zeros_like(enter)
    gain[...] = jnp.ones_like(gain)
    for d in range(1, QUAD):

        @pl.when(place >= d)
        def _():
            for copy in b_copies[d - 1]:
                copy.wait_recv()
            enter[...] += gain[...] * trecv[d - 1].astype(F32)
            gain[...] = gain[...] * ktrecv[d - 1]

    @pl.when(zlo == QUAD - 1)
    def _():
        usend[...] = (run_k * enter[...] + run_v).astype(BF16)
        for copy in u_copies:
            copy.start()

    for d in range(1, QUAD + 1):

        @pl.when(zlo == QUAD - 1 + d)
        def _():
            u_copies[d - 1].wait_recv()
            enter[...] += gain[...] * urecv[...].astype(F32)

    for b in range(GROUP):
        inner_k, inner_v = inner[b]
        csend[b] = (inner_k * enter[...] + inner_v).astype(BF16)
    c_copies = []
    for j in (2, 6, 4, 1, 7, 3, 5):
        other, target = in_group(j)
        c_copies.append(
            remote(csend.at[other], mem.at[slice_rows], cs_sem.at[j], cr_sem.at[j], target)
        )
        c_copies[-1].start()
    mem[slice_rows, :] = csend[r]

    @pl.when(seq > 0)
    def _():
        for copy in kv_copies:
            copy.wait_recv()
        vt[...] = vprev[...].T
        for h in range(2):
            for t in range(TOK // TILE):
                token_part(kprev, vt, h, t, t * TILE, TOK, True, False)

    for copy in c_copies:
        copy.wait_recv()
    mem_t = mem[...].T
    x_rows = pl.ds(pl.multiple_of(x * COLS, COLS), COLS)
    x_copies = []
    for n in range(NCHUNK):
        toks = slice(n * CHUNK, (n + 1) * CHUNK)
        for h in range(2):
            cols = slice(h * HEAD, (h + 1) * HEAD)
            scores = nt(mem[:, cols], q[toks, cols]) * EXP2_SCALE
            before = top[h, :, toks]
            highest = jnp.maximum(jnp.max(scores, axis=0, keepdims=True), before)
            fade = jnp.exp2(before - highest)
            weights = jnp.exp2(scores - highest)
            sums = fade * total[h, :, toks] + jnp.sum(weights, axis=0, keepdims=True)
            summed = fade * acc[cols, toks] + nn(mem_t[cols, :], weights.astype(BF16))
            xatt[n, pl.ds(pl.multiple_of(x * COLS + h * HEAD, HEAD), HEAD), :] = (
                summed / sums
            ).astype(BF16)
        sent = []
        for j in (1, 3, 2):
            _, target = on_x(j)
            sent.append(
                remote(
                    xatt.at[n, x_rows], xatt.at[n, x_rows], xs_sem.at[n, j], xr_sem.at[n, j], target
                )
            )
            sent[-1].start()
        x_copies.append(sent)

    pl.semaphore_wait(ready.at[2], 2)
    for copy in w_loads:
        copy.wait()
    for copy in w_copies:
        copy.wait_recv()
    z_copies = []
    for n in range(NCHUNK):
        for copy in x_copies[n]:
            copy.wait_recv()
        zsend[n] = nn(wbuf[1], xatt[n]).astype(BF16)
        z_copies.append(remote(zsend.at[n], zrecv.at[n], zs_sem.at[n], zr_sem.at[n], partner))
        z_copies[-1].start()
    for n in range(NCHUNK):
        own[n] = nn(wbuf[0], xatt[n])
    for n in range(NCHUNK):
        z_copies[n].wait_recv()
        o_ref[:, n * CHUNK : (n + 1) * CHUNK] = (own[n] + zrecv[n].astype(F32)).astype(BF16)

    for copy in a_copies + w_copies + c_copies + z_copies:
        copy.wait_send()
    for sent in x_copies:
        for copy in sent:
            copy.wait_send()

    @pl.when(seq < 63)
    def _():
        for copy in kv_copies:
            copy.wait_send()

    for d in range(1, QUAD):

        @pl.when(place + d < QUAD)
        def _():
            for copy in b_copies[d - 1]:
                copy.wait_send()

    @pl.when(zlo == QUAD - 1)
    def _():
        for copy in u_copies:
            copy.wait_send()


def body(queries, key_rows, value_rows, slot_queries, gate_logit, out_weight):
    dma = pltpu.SemaphoreType.DMA
    vmem = pltpu.VMEM
    return pl.pallas_call(
        kernel,
        out_shape=pltpu.VMEM((ROWS, TOK), BF16),
        in_specs=[pl.BlockSpec(memory_space=pl.ANY)] * 6,
        out_specs=pl.BlockSpec(memory_space=pltpu.VMEM),
        scratch_shapes=[
            vmem((TOK, COLS), BF16),
            vmem((TOK, COLS), BF16),
            vmem((TOK, COLS), BF16),
            vmem((STATE, COLS), BF16),
            vmem((COLS, TOK), BF16),
            vmem((TOK, COLS), BF16),
            vmem((TOK, COLS), BF16),
            vmem((1, COLS), F32),
            vmem((GROUP, SLICE + EXTRA, COLS), BF16),
            vmem((GROUP, SLICE + EXTRA, COLS), BF16),
            vmem((SLICE, COLS), BF16),
            vmem((QUAD - 1, SLICE, COLS), BF16),
            vmem((1, COLS), F32),
            vmem((QUAD - 1, 1, COLS), F32),
            vmem((SLICE, COLS), BF16),
            vmem((SLICE, COLS), BF16),
            vmem((SLICE, COLS), F32),
            vmem((1, COLS), F32),
            vmem((GROUP, SLICE, COLS), BF16),
            vmem((STATE, COLS), BF16),
            vmem((2, ROWS, XS * COLS), BF16),
            vmem((2, 1, TOK), F32),
            vmem((2, 1, TOK), F32),
            vmem((COLS, TOK), F32),
            vmem((NCHUNK, XS * COLS, CHUNK), BF16),
            vmem((NCHUNK, ROWS, CHUNK), BF16),
            vmem((NCHUNK, ROWS, CHUNK), BF16),
            vmem((NCHUNK, ROWS, CHUNK), F32),
            dma((5,)),
            dma((2,)),
            dma((GROUP,)),
            dma((GROUP,)),
            dma((2,)),
            dma((2,)),
            dma((XS, 2)),
            dma((XS, 2)),
            dma((QUAD - 1,)),
            dma((QUAD - 1,)),
            dma((QUAD - 1,)),
            dma((QUAD - 1,)),
            dma((QUAD,)),
            dma((QUAD,)),
            dma((GROUP,)),
            dma((GROUP,)),
            dma((NCHUNK, XS)),
            dma((NCHUNK, XS)),
            dma((NCHUNK,)),
            dma((NCHUNK,)),
            pltpu.SemaphoreType.REGULAR((3,)),
        ],
        compiler_params=pltpu.CompilerParams(collective_id=0, has_side_effects=True),
    )(queries, key_rows, value_rows, slot_queries, gate_logit, out_weight)


def solution(mesh):
    in_specs = (
        P("seq", "dp"),
        P("seq", "dp"),
        P("seq", "dp"),
        P(None, "dp"),
        P("seq", "dp"),
        P(None, "dp"),
    )
    return jax.shard_map(
        body, mesh=mesh, in_specs=in_specs, out_specs=P("dp", "seq"), check_vma=False
    )
```
